256 devices in a mesh: row: 8 (over y, core), col: 32 (over z, x).
Axes of the slice: x: 4, y: 4, z: 8, core: 2. Of those that a mesh axis runs over, the one named last changes fastest.
Arguments:
- embeds: bfloat16 [3072, 8192], P('row', 'col'), may hold values from -600 to 600
- ln_gain: float32 [8192], replicated, may hold values from 0.1 to 1.9
- ln_bias: float32 [8192], replicated, may hold values from -3 to 3
- w_qkv: bfloat16 [8192, 24576], P('row', 'col'), may hold values from -4 to 4, as said below
- w_out: bfloat16 [8192, 8192], P('row', 'col'), may hold values from -0.0625 to 0.0625
- out_bias: float32 [8192], P('col'), may hold values from -3 to 3
Outputs:
- attended: bfloat16 [3072, 8192], P('row', 'col')
The draws below stay inside these ranges and needn't reach their ends.
Inputs may be any that keep to these rules, and one draw needn't show every extreme that they name: Columns of w_qkv are ordered by head, then query, key, value, then entry of the head.
All inputs are finite; a program needn't handle non-finite values.
Results may differ from the reference program's by a relative error of at most 0.0065.
Values may be sent and summed in bfloat16 or wider, within the bound.
A program may use at most 64 MiB of HBM per device.

```python
import jax
import jax.numpy as jnp
from jax import lax

D = 8192
HEADS = 64
SEQ = 128
TOK_DEV = 384
N_ROW = 8


def draw_embeds(key, part):
    keys = jax.random.split(jax.random.fold_in(key, 11), 4)
    rows = TOK_DEV * N_ROW
    noise = jnp.clip(jax.random.normal(keys[0], (rows, D), jnp.float32), -4.0, 4.0)
    row_scale = jnp.exp(jax.random.uniform(keys[1], (rows, 1), jnp.float32, 0.0, jnp.log(10.0)))
    offset = jax.random.uniform(keys[2], (rows, 1), jnp.float32, -2.0, 2.0)
    ramp = jnp.power(10.0, jnp.arange(D, dtype=jnp.float32) / D)
    col_scale = ramp * jnp.exp(jax.random.uniform(keys[3], (D,), jnp.float32, jnp.log(0.7), jnp.log(1.4)))
    values = row_scale * (offset + noise * col_scale)
    return values.astype(jnp.bfloat16)


def draw_w_qkv(key, part):
    keys = jax.random.split(jax.random.fold_in(key, 23), 1)
    head_size = D // HEADS
    weights = jax.random.normal(keys[0], (D, HEADS, 3, head_size), jnp.float32) * D ** (-0.5)
    weights = jnp.clip(weights, -4.0, 4.0)
    return weights.reshape(D, 3 * D).astype(jnp.bfloat16)


def levels(own_key, dims, cuts, least, largest):
    gain, own = 1.0, jax.random.fold_in(own_key, 6)
    for axis_at, parts in cuts:
        heights = jnp.exp(jax.random.uniform(jax.random.fold_in(own, axis_at), (parts,), jnp.float32, least / len(cuts), largest / len(cuts)))
        gain = gain * jnp.repeat(heights, dims[axis_at] // parts).reshape([-1 if axis == axis_at else 1 for axis in range(len(dims))])
    return gain


def bell_draw(key, dims, deviation, reach, cuts=(), held_as=jnp.bfloat16):
    loudness = levels(key, dims, cuts, -0.22, 0.18) if cuts else 1.0
    values = jax.random.normal(key, dims, jnp.float32) * deviation * loudness
    return jnp.minimum(jnp.maximum(values, -reach), reach).astype(held_as)


def setup_inputs(seed: int = 0) -> dict:
    key_of = jax.random.split(jax.random.key(seed), 7)
    embeds = draw_embeds(jax.random.fold_in(key_of[6], 71), 0)
    ln_gain = jnp.clip(1.0 + 0.18 * jax.random.normal(key_of[1], (D,), jnp.float32), 0.1, 1.9)
    ln_bias = bell_draw(key_of[2], (D,), 0.5, 3.0, (), jnp.float32)
    w_qkv = draw_w_qkv(jax.random.fold_in(key_of[6], 71), 0)
    w_out = bell_draw(key_of[4], (D, D), D ** -0.5, 0.0625, ((0, 8), (1, 32)))
    out_bias = bell_draw(key_of[5], (D,), 0.5, 3.0, ((0, 32),), jnp.float32)
    return dict(embeds=embeds, ln_gain=ln_gain, ln_bias=ln_bias, w_qkv=w_qkv, w_out=w_out, out_bias=out_bias)


def reference(embeds, ln_gain, ln_bias, w_qkv, w_out, out_bias):
    values = embeds.astype(jnp.float32)
    mean = lax.optimization_barrier(jnp.mean(values, axis=1, keepdims=True))
    var = lax.optimization_barrier(jnp.mean((values - mean) ** 2, axis=1, keepdims=True))
    normed = ((values - mean) * jax.lax.rsqrt(var + 1e-05) * ln_gain + ln_bias).astype(jnp.bfloat16)
    qkv = jnp.dot(normed, w_qkv, preferred_element_type=jnp.float32).astype(jnp.bfloat16)
    total = qkv.shape[0]
    head_size = D // HEADS
    packed = qkv.astype(jnp.float32).reshape(total // SEQ, SEQ, HEADS, 3, head_size)
    query = packed[:, :, :, 0]
    keys = packed[:, :, :, 1]
    vals = packed[:, :, :, 2]
    scores = jnp.einsum('nqhd,nkhd->nhqk', query, keys) / jnp.sqrt(jnp.float32(head_size))
    peak = lax.optimization_barrier(jnp.max(scores, axis=-1, keepdims=True))
    expo = jnp.exp(scores - peak)
    probs = (expo / lax.optimization_barrier(jnp.sum(expo, axis=-1, keepdims=True))).astype(jnp.bfloat16)
    context = jnp.einsum('nhqk,nkhd->nqhd', probs.astype(jnp.float32), vals).astype(jnp.bfloat16)
    context = context.reshape(total, D)
    result = jnp.dot(context, w_out, preferred_element_type=jnp.float32) + out_bias
    return result.astype(jnp.bfloat16)
```

```python
import jax
import jax.numpy as jnp
from jax import lax
from jax.sharding import PartitionSpec as P

D = 8192
HEADS = 64
SEQ = 128


def normalize(values, mean, var, gain, shift):
    return ((values - mean) * lax.rsqrt(var + 1e-05) * gain + shift).astype(jnp.bfloat16)


def attend(qkv):
    total, columns = qkv.shape
    head_size = D // HEADS
    heads = columns // (3 * head_size)
    packed = qkv.reshape(total // SEQ, SEQ, heads, 3, head_size)
    query = packed[:, :, :, 0]
    keys = packed[:, :, :, 1]
    vals = packed[:, :, :, 2]
    scores = jnp.einsum("nqhd,nkhd->nhqk", query, keys, preferred_element_type=jnp.float32)
    scores = scores / jnp.sqrt(jnp.float32(head_size))
    peak = jnp.max(scores, axis=-1, keepdims=True)
    expo = jnp.exp(scores - peak)
    probs = (expo / jnp.sum(expo, axis=-1, keepdims=True)).astype(jnp.bfloat16)
    context = jnp.einsum("nhqk,nkhd->nqhd", probs, vals, preferred_element_type=jnp.float32)
    return context.astype(jnp.bfloat16).reshape(total, heads * head_size)


def on_device(embeds, ln_gain, ln_bias, w_qkv, w_out, out_bias):
    values = lax.all_gather(embeds, "col", axis=1, tiled=True).astype(jnp.float32)
    mean = jnp.mean(values, axis=1, keepdims=True)
    var = jnp.mean((values - mean) ** 2, axis=1, keepdims=True)
    gathered = normalize(values, mean, var, ln_gain, ln_bias)
    left = gathered
    qkv = jnp.dot(
        left, lax.all_gather(w_qkv, "row", axis=0, tiled=True), preferred_element_type=jnp.float32
    )
    context = attend(qkv.astype(jnp.bfloat16))
    full_context = lax.all_gather(context, "col", axis=1, tiled=True)
    left = full_context
    result = jnp.dot(
        left, lax.all_gather(w_out, "row", axis=0, tiled=True), preferred_element_type=jnp.float32
    )
    return (result + out_bias).astype(jnp.bfloat16)


def solution(mesh):
    return jax.shard_map(
        on_device,
        mesh=mesh,
        in_specs=(P("row", "col"), P(), P(), P("row", "col"), P("row", "col"), P("col")),
        out_specs=P("row", "col"),
        check_vma=False,
    )
```

```python
import functools
import heapq

import jax
import jax.numpy as jnp
from jax import lax
from jax.experimental import pallas as pl
from jax.experimental.pallas import tpu as pltpu
from jax.sharding import PartitionSpec as P

D = 8192
SEQ = 128
HEAD = 128
TOK = 384
WIDTH = 256
NX, NY, NZ = 4, 4, 8
CUT = 160
WQ = 4
QROWS = 1024 // WQ
MESH = pl.DeviceIdType.MESH


class Plan:
    def __init__(self):
        self.copies = {}
        self.steps = {}

    def copy(self, name, link, size, src, dst, landed, needs=(), level=0):
        self.copies[name] = dict(
            name=name, link=link, size=size, src=src, dst=dst, landed=landed, needs=tuple(needs), level=level,
            index=len(self.copies),
        )

    def step(self, name, cost, run, needs=(), level=0):
        self.steps[name] = dict(name=name, cost=cost, run=run, needs=tuple(needs), level=level)

    def order(self, rate, lag):
        now, when, free = 0.0, {}, {}
        waiting = {**self.copies, **self.steps}
        result = []
        while waiting:
            best = None
            for name, item in waiting.items():
                times = [when.get(need) for need in item["needs"]]
                if any(t is None for t in times):
                    continue
                ready = max(times, default=0.0)
                key = (max(ready, now), item["level"], ready, name in self.steps)
                if best is None or key < best[0]:
                    best = (key, name)
            key, name = best
            item = waiting.pop(name)
            now = key[0]
            result.append(name)
            if name in self.steps:
                now += item["cost"]
                when[name] = now
            else:
                now += 0.03
                link = item["link"]
                begin = max(now, free.get(link, 0.0))
                free[link] = begin + item["size"] / rate[link[0]]
                when[name] = free[link] + lag[link[0]]
        self.when = when
        return result


def ring(plan, axis, n, tag, block, rows, size, needs, level):
    low, high = rows
    middle = (low + high) // 2
    done = {0: list(needs)}
    for sign, mark in ((-1, "p"), (1, "m")):
        previous = list(needs)
        for hop in range(1, n // 2 + 1):
            half = hop == n // 2
            part = ((low, middle) if mark == "p" else (middle, high)) if half else rows
            name = f"{tag}.{axis}{mark}{hop}"
            plan.copy(
                name, axis + mark, size * (part[1] - part[0]),
                block(sign * (hop - 1), part), block(sign * (hop - 1), part), block(sign * hop, part),
                previous, level,
            )
            previous = [name]
            done.setdefault((sign * hop) % n, []).append(name)
    return done


def gather(plan, tag, slot, size, needs, level):
    done = {offset: [] for offset in range(NZ)}
    first, second = (0, CUT), (CUT, TOK)
    across = ring(plan, "x", NX, tag + "a", lambda o, r: functools.partial(slot, 0, o, r), first, size, needs, level)
    along = ring(plan, "z", NZ, tag + "b", lambda o, r: functools.partial(slot, o, 0, r), second, size, needs, level)
    for at, arrivals in across.items():
        found = ring(
            plan, "z", NZ, f"{tag}a{at}", lambda o, r, at=at: functools.partial(slot, o, at, r), first, size, arrivals, level
        )
        for offset, names in found.items():
            done[offset] += names
    for at, arrivals in along.items():
        found = ring(
            plan, "x", NX, f"{tag}b{at}", lambda o, r, at=at: functools.partial(slot, at, o, r), second, size, arrivals, level
        )
        for names in found.values():
            done[at] += names
    return done


def to_columns(row):
    return jnp.transpose(jnp.broadcast_to(row, (128, TOK)))


def kernel(embeds, gain, shift, w_qkv, w_out, out_bias, out, normed, wide, last, ctx, total, sums, stat_x, stat_z,
           send_sem, recv_sem, own_sem):
    row, col = lax.axis_index("row"), lax.axis_index("col")
    y, core = row // 2, row % 2
    z, x = col // NX, col % NX

    def at(dx=0, dy=0, dz=0, other=0):
        their_core = 1 - core if other else core
        return (2 * ((y + dy + NY) % NY) + their_core, NX * ((z + dz + NZ) % NZ) + (x + dx + NX) % NX)

    near = dict(
        xp=at(dx=1), xm=at(dx=-1), yp=at(dy=1), ym=at(dy=-1), zp=at(dz=1), zm=at(dz=-1), c=at(other=1)
    )
    for d in range(1, NX):
        near[f"sx{d}"] = at(dx=d)
    for d in range(1, NZ):
        near[f"sz{d}"] = at(dz=d)

    plan = Plan()

    lines = lax.broadcasted_iota(jnp.int32, (8, TOK), 0)

    def pack(total_, spread):
        return jnp.where(lines == 0, total_, jnp.where(lines == 1, spread, 0.0))

    def merge(stats, n, count):
        totals = [stats[i][0:1] for i in range(n)]
        full = functools.reduce(jnp.add, totals)
        mean = full * (1.0 / (n * count))
        spread = functools.reduce(jnp.add, [stats[i][1:2] for i in range(n)])
        apart = functools.reduce(jnp.add, [(t * (1.0 / count) - mean) ** 2 for t in totals])
        return full, mean, spread + count * apart

    def stats_own():
        values = embeds[...].astype(jnp.float32)
        summed = jnp.sum(values, axis=1, keepdims=True)
        apart = values - summed * (1.0 / WIDTH)
        spread = jnp.sum(apart * apart, axis=1, keepdims=True)
        lane = lax.broadcasted_iota(jnp.int32, (TOK, 128), 1)
        both = jnp.where(lane == 0, summed, jnp.where(lane == 1, spread, 0.0))
        stat_x[x] = jnp.transpose(both)[0:8]

    def stats_x():
        full, _, spread = merge(stat_x, NX, WIDTH)
        stat_z[z] = pack(full, spread)

    def norm():
        _, mean, spread = merge(stat_z, NZ, NX * WIDTH)
        scale = lax.rsqrt(spread * (1.0 / D) + 1e-05)
        mean, scale = to_columns(mean), to_columns(scale)
        mean, scale = jnp.concatenate([mean] * 2, axis=1), jnp.concatenate([scale] * 2, axis=1)
        columns = pl.ds(pl.multiple_of(col * WIDTH, WIDTH), WIDTH)
        values = embeds[...].astype(jnp.float32)
        values = (values - mean) * scale * gain[:, columns] + shift[:, columns]
        normed[z, x] = values.astype(jnp.bfloat16)

    for d in range(1, NX):
        plan.copy(
            f"sx{d}", f"sx{d}", 12288, lambda: stat_x.at[x], lambda: stat_x.at[x],
            lambda d=d: stat_x.at[(x - d + NX) % NX], (), -2,
        )
    plan.step("stats_x", 0.3, stats_x, [f"sx{d}" for d in range(1, NX)], -2)
    for d in range(1, NZ):
        plan.copy(
            f"sz{d}", f"sz{d}", 12288, lambda: stat_z.at[z], lambda: stat_z.at[z],
            lambda d=d: stat_z.at[(z - d + NZ) % NZ], ("stats_x",), -2,
        )
    plan.step("norm", 1.0, norm, [f"sz{d}" for d in range(1, NZ)], -2)

    def weights(tag, own, slot, count, unit, gate, level):
        whole, names = (0, count), []
        gate = list(gate)
        for mark, sign in (("p", -1), ("m", 1)):
            part = (0, count // 2) if mark == "p" else (count // 2, count)
            first, second = f"{tag}.y{mark}1", f"{tag}.y{mark}2"
            plan.copy(first, "y" + mark, count * unit, own, functools.partial(slot, 0, core, whole),
                      functools.partial(slot, sign, core, whole), gate, level)
            there = functools.partial(slot, sign, core, part)
            plan.copy(second, "y" + mark, (part[1] - part[0]) * unit, there, there,
                      functools.partial(slot, 2 * sign, core, part), [first], level)
            for name, offset, rows in ((first, sign, whole), (second, 2 * sign, part)):
                here = functools.partial(slot, offset, core, rows)
                plan.copy(name + "c", "c", (rows[1] - rows[0]) * unit, here, here,
                          functools.partial(slot, offset, 1 - core, rows), [name], level)
                names += [name, name + "c"]
        plan.copy(tag + ".c", "c", count * unit, own, functools.partial(slot, 0, core, whole),
                  functools.partial(slot, 0, 1 - core, whole), gate, level)
        return names + [tag + ".c"]

    def wide_slot(head, piece, dy, their_core, rows):
        r = 2 * ((y + dy + NY) % NY) + their_core
        return wide.at[r, head, pl.ds(piece * QROWS + rows[0], rows[1] - rows[0]), :]

    def last_slot(head, dy, their_core, rows):
        r = 2 * ((y + dy + NY) % NY) + their_core
        return last.at[r, head, pl.ds(rows[0], rows[1] - rows[0])]

    need_w, gates = {}, [[], []]
    for head in range(2):
        for piece in range(WQ):
            tag = f"w{head}{piece}"
            own = lambda head=head, piece=piece: w_qkv.at[pl.ds(piece * QROWS, QROWS), pl.ds(head * 384, 384)]
            need_w[head, piece] = weights(
                tag, own, functools.partial(wide_slot, head, piece), QROWS, 768, gates[-2], 0
            )
            gates.append([tag + ".yp1", tag + ".ym1"])
    need_o = {}
    for head in range(2):
        tag = f"o{head}"
        own = lambda head=head: w_out.at[:, head]
        need_o[head] = weights(tag, own, functools.partial(last_slot, head), 4, HEAD * WIDTH * 2, gates[-2], 0)
        gates.append([tag + ".yp1", tag + ".ym1"])

    def normed_slot(dz, dx, rows):
        return normed.at[(z + dz + NZ) % NZ, (x + dx + NX) % NX, pl.ds(rows[0], rows[1] - rows[0]), :]

    need_e = gather(plan, "e", normed_slot, WIDTH * 2, ["norm"], 0)

    def project(head, offset):
        r = (z + offset) % NZ
        left = jnp.concatenate([normed[r, i] for i in range(NX)], axis=1)
        product = jnp.dot(left, wide[r, head], preferred_element_type=jnp.float32)
        if offset == 0:
            total[...] = product
        else:
            total[...] += product

    def project_piece(piece):
        def body(r, carry):
            rows = pl.ds(piece * QROWS, QROWS)
            total[...] += jnp.dot(normed[r, piece], wide[r, 1, rows, :], preferred_element_type=jnp.float32)
            return carry

        if piece == 0:
            total[...] = jnp.zeros_like(total)
        lax.fori_loop(0, 8, body, 0)

    def attend(head):
        qkv = total[...].astype(jnp.bfloat16)
        for s in range(TOK // SEQ):
            part = qkv[s * SEQ:(s + 1) * SEQ]
            query, keys, vals = part[:, :HEAD], part[:, HEAD:2 * HEAD], part[:, 2 * HEAD:]
            scores = lax.dot_general(query, keys, (((1,), (1,)), ((), ())), preferred_element_type=jnp.float32)
            scores = scores * (HEAD ** -0.5)
            expo = jnp.exp(scores - jnp.max(scores, axis=-1, keepdims=True))
            probs = (expo / jnp.sum(expo, axis=-1, keepdims=True)).astype(jnp.bfloat16)
            mixed = jnp.dot(probs, vals, preferred_element_type=jnp.float32)
            ctx[head, z, x, pl.ds(s * SEQ, SEQ), :] = mixed.astype(jnp.bfloat16)

    def output(head, offset):
        r = (z + offset) % NZ
        left = jnp.concatenate([ctx[head, r, i] for i in range(NX)], axis=1)
        right = last[r, head].reshape(NX * HEAD, WIDTH)
        product = jnp.dot(left, right, preferred_element_type=jnp.float32)
        if head == 0 and offset == 0:
            sums[...] = product + out_bias[...]
        else:
            sums[...] += product

    walk = [0, 1, 7, 2, 6, 3, 5, 4]
    w0 = [name for piece in range(WQ) for name in need_w[0, piece]]
    before = []
    for offset in walk:
        plan.step(f"p0{offset}", 0.7, functools.partial(project, 0, offset), w0 + need_e[offset] + before, 1)
        before = [f"p0{offset}"]
    plan.step("a0", 1.5, functools.partial(attend, 0), before, 1)
    before = ["a0"] + [name for offset in walk for name in need_e[offset]]
    for piece in range(WQ):
        plan.step(f"p1{piece}", 1.3, functools.partial(project_piece, piece), need_w[1, piece] + before, 1)
        before = [f"p1{piece}"]
    plan.step("a1", 1.5, functools.partial(attend, 1), before, 1)

    for head in range(2):
        def ctx_slot(dz, dx, rows, head=head):
            return ctx.at[head, (z + dz + NZ) % NZ, (x + dx + NX) % NX, pl.ds(rows[0], rows[1] - rows[0]), :]

        need_c = gather(plan, f"c{head}", ctx_slot, HEAD * 2, [f"a{head}"], 0)
        before = [f"f{head - 1}{walk[-1]}"] if head else []
        for offset in walk:
            plan.step(
                f"f{head}{offset}", 0.3, functools.partial(output, head, offset),
                need_o[head] + need_c[offset] + before, 2,
            )
            before = [f"f{head}{offset}"]

    rate = dict(x=49e3, y=49e3, z=49e3, c=500e3, s=49e3)
    lag = dict(x=1.6, y=1.6, z=1.6, c=1.0, s=4.0)
    order = plan.order(rate, lag)

    def make(item, landed=False):
        index = item["index"]
        return pltpu.make_async_remote_copy(
            src_ref=(item["landed"] if landed else item["src"])(),
            dst_ref=(item["landed"] if landed else item["dst"])(),
            send_sem=send_sem.at[index], recv_sem=recv_sem.at[index],
            device_id=near[item["link"]], device_id_type=MESH,
        )

    barrier = pltpu.get_barrier_semaphore()
    partners = {k: v for k, v in near.items() if k not in ("sx1", "sx3", "sz1", "sz7")}
    for device in partners.values():
        pl.semaphore_signal(barrier, inc=1, device_id=device, device_id_type=MESH)
    own = [
        pltpu.make_async_copy(w_qkv.at[:, pl.ds(0, 384)], wide.at[row, 0], own_sem.at[0]),
        pltpu.make_async_copy(w_qkv.at[:, pl.ds(384, 384)], wide.at[row, 1], own_sem.at[1]),
        pltpu.make_async_copy(w_out.at[:, 0], last.at[row, 0], own_sem.at[2]),
        pltpu.make_async_copy(w_out.at[:, 1], last.at[row, 1], own_sem.at[3]),
    ]
    for item in own:
        item.start()
    stats_own()
    pl.semaphore_wait(barrier, len(partners))

    seen = set()
    used_own = False
    for name in order:
        item = plan.copies.get(name) or plan.steps[name]
        for need in item["needs"]:
            if need in plan.copies and need not in seen:
                seen.add(need)
                make(plan.copies[need], landed=True).wait_recv()
        if name in plan.copies:
            make(item).start()
        else:
            if name[0] == "p" and not used_own:
                used_own = True
                for copy in own:
                    copy.wait()
            item["run"]()
    for name, item in plan.copies.items():
        if name not in seen:
            make(item, landed=True).wait_recv()
    for item in plan.copies.values():
        make(item).wait_send()
    out[...] = sums[...].astype(jnp.bfloat16)


COPIES = 3 + 7 + 9 * (2 * WQ + 2) + 3 * (4 + 8 + 4 * 8 + 8 * 4)


def on_device(embeds, ln_gain, ln_bias, w_qkv, w_out, out_bias):
    vmem = pl.BlockSpec(memory_space=pltpu.VMEM)
    anywhere = pl.BlockSpec(memory_space=pl.ANY)
    bf16, f32 = jnp.bfloat16, jnp.float32
    return pl.pallas_call(
        kernel,
        out_shape=jax.ShapeDtypeStruct((TOK, WIDTH), bf16),
        in_specs=[vmem, vmem, vmem, anywhere, anywhere, vmem],
        out_specs=vmem,
        scratch_shapes=[
            pltpu.VMEM((NZ, NX, TOK, WIDTH), bf16),
            pltpu.VMEM((8, 2, 1024, 384), bf16),
            pltpu.VMEM((8, 2, NX, HEAD, WIDTH), bf16),
            pltpu.VMEM((2, NZ, NX, TOK, HEAD), bf16),
            pltpu.VMEM((TOK, 384), f32),
            pltpu.VMEM((TOK, WIDTH), f32),
            pltpu.VMEM((NX, 8, TOK), f32),
            pltpu.VMEM((NZ, 8, TOK), f32),
            pltpu.SemaphoreType.DMA((COPIES,)),
            pltpu.SemaphoreType.DMA((COPIES,)),
            pltpu.SemaphoreType.DMA((4,)),
        ],
        compiler_params=pltpu.CompilerParams(
            collective_id=0, has_side_effects=True, vmem_limit_bytes=60 * 1024 * 1024
        ),
        name="block",
    )(
        embeds, ln_gain.reshape(1, D), ln_bias.reshape(1, D), w_qkv,
        w_out.reshape(NX, 2, HEAD, WIDTH), out_bias.reshape(1, WIDTH),
    )


def solution(mesh):
    return jax.shard_map(
        on_device,
        mesh=mesh,
        in_specs=(P("row", "col"), P(), P(), P("row", "col"), P("row", "col"), P("col")),
        out_specs=P("row", "col"),
        check_vma=False,
    )
```

```python
import functools
import heapq

import jax
import jax.numpy as jnp
from jax import lax
from jax.experimental import pallas as pl
from jax.experimental.pallas import tpu as pltpu
from jax.sharding import PartitionSpec as P

D = 8192
SEQ = 128
HEAD = 128
TOK = 384
WIDTH = 256
NX, NY, NZ = 4, 4, 8
EARLY = ((0, 96, 256), (256, 320, 384))
LATE = ((0, 96, 256), (256, 320, 384))
AHEAD = 3
WQ = 8
QROWS = 1024 // WQ
MESH = pl.DeviceIdType.MESH


class Plan:
    def __init__(self):
        self.copies = {}
        self.groups = {}
        self.steps = {}

    def copy(self, name, link, size, src, dst, group, sent, needs=(), level=0):
        self.copies[name] = dict(
            link=link, size=size, src=src, dst=dst, group=group, sent=sent, needs=tuple(needs), level=level
        )
        if group not in self.groups:
            self.groups[group] = dict(index=len(self.groups), size=0)
        self.groups[group]["size"] += size

    def step(self, name, cost, run, needs=(), level=0):
        self.steps[name] = dict(cost=cost, run=run, needs=tuple(needs), level=level)

    def order(self, rate, lag):
        now, when, free, left = 0.0, {}, {}, {}
        for item in self.copies.values():
            left[item["group"]] = left.get(item["group"], 0) + 1
        landed = {}
        waiting = {**self.copies, **self.steps}
        result = []
        while waiting:
            best = None
            for name, item in waiting.items():
                times = [when.get(need) for need in item["needs"]]
                if any(t is None for t in times):
                    continue
                ready = max(times, default=0.0)
                if "link" in item:
                    ready = max(ready, free.get(item["link"], 0.0) - QUEUE)
                key = (max(ready - item.get("eager", 0.0), now), item["level"], ready, name in self.steps)
                if best is None or key < best[0]:
                    best = (key, name)
            key, name = best
            item = waiting.pop(name)
            now = max(now, key[2])
            result.append(name)
            if name in self.steps:
                now += item["cost"]
                when[name] = now
            else:
                now += 0.01
                link, group = item["link"], item["group"]
                begin = max(now, free.get(link, 0.0))
                free[link] = begin + item["size"] / rate[link[0]]
                landed[group] = max(landed.get(group, 0.0), free[link] + lag[link[0]])
                left[group] -= 1
                if not left[group]:
                    when[group] = landed[group]
        self.when = when
        return result


def halves(rows, mark):
    low, high = rows
    middle = (low + high) // 2
    return (low, middle) if mark == "p" else (middle, high)


def ring(plan, axis, n, tag, classes, slot, rows, size, needs, level, after=0, last=None):
    done = {0: list(needs)}
    for hop in range(1, n // 2 + 1):
        group = last if last and hop == n // 2 else f"{tag}_{hop}"
        for place in classes:
            for sign, mark in ((-1, "p"), (1, "m")):
                part = halves(rows, mark) if hop == n // 2 else rows
                place_of = (place, sign * (hop - 1), part)
                plan.copy(
                    f"{tag}_{place}{mark}{hop}", axis + mark, size * (part[1] - part[0]),
                    functools.partial(slot, *place_of, True), functools.partial(slot, *place_of, False), group,
                    tag[:2], done[hop - 1], level - HOP * (n // 2 - hop + after),
                )
        done[hop] = [group]
    return done


def gather(plan, tag, slot, part, size, needs, level, merged=0):
    first, second = part[:2], part[1:]
    found = {distance: [] for distance in range(NZ // 2 + 1)}
    ends = lambda distance: f"{tag}z" if distance < merged else None
    along_x = lambda place, offset, rows, src: slot(place, offset, rows, src)
    along_z = lambda place, offset, rows, src: slot(offset, place, rows, src)
    pairs = lambda distance, n: sorted({distance, (n - distance) % n})
    across = ring(plan, "x", NX, tag + "a", [0], along_x, first, size, needs, level, NZ // 2)
    along = ring(plan, "z", NZ, tag + "b", [0], along_z, second, size, needs, level, NX // 2)
    for distance in range(NX // 2 + 1):
        done = ring(plan, "z", NZ, f"{tag}a{distance}", pairs(distance, NX), along_z, first, size, across[distance],
                    level, 0, ends(NZ // 2) or f"{tag}al")
        for hop, names in done.items():
            found[hop] += names
    for distance in range(NZ // 2 + 1):
        done = ring(plan, "x", NX, f"{tag}b{distance}", pairs(distance, NZ), along_x, second, size, along[distance],
                    level, 0, ends(distance))
        for names in done.values():
            found[distance] += names
    return found


def to_columns(row):
    wide = jnp.transpose(jnp.broadcast_to(row, (128, TOK)))
    return jnp.concatenate([wide] * (WIDTH // 128), axis=1)


def kernel(embeds, gain, shift, w_qkv, w_out, out_bias, out, raw, normed, wide, last, ctx, total, sums, mean_cols,
           scale_cols, stat_x, stat_z, send_sem, recv_sem, own_sem):
    row, col = lax.axis_index("row"), lax.axis_index("col")
    y, core = row // 2, row % 2
    z, x = col // NX, col % NX

    def at(dx=0, dy=0, dz=0, other=0):
        their_core = 1 - core if other else core
        return (2 * ((y + dy + NY) % NY) + their_core, NX * ((z + dz + NZ) % NZ) + (x + dx + NX) % NX)

    near = dict(
        xp=at(dx=1), xm=at(dx=-1), yp=at(dy=1), ym=at(dy=-1), zp=at(dz=1), zm=at(dz=-1), c=at(other=1)
    )
    for d in range(1, NX):
        near[f"sx{d}"] = at(dx=d)
    for d in range(1, NZ):
        near[f"sz{d}"] = at(dz=d)

    plan = Plan()

    lines = lax.broadcasted_iota(jnp.int32, (8, TOK), 0)

    def pack(total_, spread):
        return jnp.where(lines == 0, total_, jnp.where(lines == 1, spread, 0.0))

    def merge(stats, n, count):
        totals = [stats[i][0:1] for i in range(n)]
        full = functools.reduce(jnp.add, totals)
        mean = full * (1.0 / (n * count))
        spread = functools.reduce(jnp.add, [stats[i][1:2] for i in range(n)])
        apart = functools.reduce(jnp.add, [(t * (1.0 / count) - mean) ** 2 for t in totals])
        return full, mean, spread + count * apart

    def stats_own():
        values = embeds[...].astype(jnp.float32)
        summed = jnp.sum(values, axis=1, keepdims=True)
        apart = values - summed * (1.0 / WIDTH)
        spread = jnp.sum(apart * apart, axis=1, keepdims=True)
        lane = lax.broadcasted_iota(jnp.int32, (TOK, 128), 1)
        both = jnp.where(lane == 0, summed, jnp.where(lane == 1, spread, 0.0))
        stat_x[x] = jnp.transpose(both)[0:8]
        raw[col] = embeds[...]

    def stats_x():
        full, _, spread = merge(stat_x, NX, WIDTH)
        stat_z[z] = pack(full, spread)

    def stats_all():
        _, mean, spread = merge(stat_z, NZ, NX * WIDTH)
        mean_cols[...] = to_columns(mean)
        scale_cols[...] = to_columns(lax.rsqrt(spread * (1.0 / D) + 1e-05))

    plan.step("stats_own", 0.8, stats_own, [], 0.5)
    for d in range(1, NX):
        plan.copy(f"sx{d}", f"sx{d}", 12288, lambda: stat_x.at[x], lambda: stat_x.at[x], "sx", "sx", ["stats_own"], -2)
    plan.step("stats_x", 0.1, stats_x, ["sx"], -2)
    for d in range(1, NZ):
        plan.copy(f"sz{d}", f"sz{d}", 12288, lambda: stat_z.at[z], lambda: stat_z.at[z], "sz", "sz", ["stats_x"], -2)
    plan.step("stats_all", 0.2, stats_all, ["sz"], -2)

    def weights(tag, own, slot, count, unit, gate, from_core):
        whole = (0, count)
        ends = [f"{tag}_1", f"{tag}_2", from_core]
        for mark, sign in (("p", -1), ("m", 1)):
            part = halves(whole, mark)
            plan.copy(f"{tag}_{mark}1", "y" + mark, count * unit, own, functools.partial(slot, 0, whole), ends[0],
                      tag[0], gate, -1)
            near_part, near_all = functools.partial(slot, sign, part), functools.partial(slot, sign, whole)
            far_part = functools.partial(slot, 2 * sign, part)
            plan.copy(f"{tag}_{mark}2", "y" + mark, (part[1] - part[0]) * unit, near_part, near_part, ends[1], tag[0],
                      ends[:1], -1)
            plan.copy(f"{tag}_{mark}1c", "c", count * unit, near_all, near_all, from_core, tag[0], ends[:1], -1)
            plan.copy(f"{tag}_{mark}2c", "c", (part[1] - part[0]) * unit, far_part, far_part, from_core, tag[0],
                      ends[1:2], -1)
        plan.copy(f"{tag}_c", "c", count * unit, own, functools.partial(slot, 0, whole), from_core, tag[0], gate, -1)
        return ends

    def wide_slot(head, piece, dy, rows):
        return wide.at[2 * ((y + dy + NY) % NY) + core, head, pl.ds(piece * QROWS + rows[0], rows[1] - rows[0]), :]

    def last_slot(head, dy, rows):
        return last.at[2 * ((y + dy + NY) % NY) + core, head, pl.ds(rows[0], rows[1] - rows[0])]

    need_w, gates = {}, [[]] * AHEAD
    first = [f"w0{WQ - 1}_1"]
    for head in range(2):
        for piece in range(WQ):
            own = lambda head=head, piece=piece: w_qkv.at[pl.ds(piece * QROWS, QROWS), pl.ds(head * 384, 384)]
            need_w[head, piece] = weights(
                f"w{head}{piece}", own, functools.partial(wide_slot, head, piece), QROWS, 768,
                first if head and piece > AHEAD and FREE else gates[-AHEAD], f"w1{piece * NX // WQ}_c" if head else "w0_c",
            )
            gates.append([f"w{head}{piece}_1"])
    need_o = {}
    for head in range(2):
        own = lambda head=head: w_out.at[:, head]
        need_o[head] = weights(
            f"o{head}", own, functools.partial(last_slot, head), 4, HEAD * WIDTH * 2, [f"w1{WQ - 1}_1"], f"o{head}_c"
        )

    def raw_slot(dz, dx, rows, src):
        if src and dz == 0 and dx == 0:
            return embeds.at[pl.ds(rows[0], rows[1] - rows[0]), :]
        return raw.at[NX * ((z + dz + NZ) % NZ) + (x + dx + NX) % NX, pl.ds(rows[0], rows[1] - rows[0]), :]

    need_e = [gather(plan, f"e{i}", raw_slot, part, WIDTH * 2, [], LEVELS[0]) for i, part in enumerate(EARLY)]

    def normalize(part, distance):
        rows = pl.ds(part[0], part[2] - part[0])
        for offset in sorted({distance, (NZ - distance) % NZ}):
            r = (z + offset) % NZ

            def body(i, carry, r=r):
                columns = pl.ds(pl.multiple_of((NX * r + i) * WIDTH, WIDTH), WIDTH)
                values = raw[NX * r + i, rows, :].astype(jnp.float32)
                values = (values - mean_cols[rows, :]) * scale_cols[rows, :] * gain[:, columns] + shift[:, columns]
                normed[r, i, rows, :] = values.astype(jnp.bfloat16)
                return carry

            lax.fori_loop(0, NX, body, 0)

    def project(part, distance):
        rows = pl.ds(part[0], part[2] - part[0])
        for offset in sorted({distance, (NZ - distance) % NZ}):
            r = (z + offset) % NZ
            left = jnp.concatenate([normed[r, i, rows, :] for i in range(NX)], axis=1)
            product = jnp.dot(left, wide[r, 0], preferred_element_type=jnp.float32)
            if offset == 0:
                total[rows, :] = product
            else:
                total[rows, :] += product

    def project_piece(piece):
        rows = pl.ds(piece * WIDTH, WIDTH)
        for some in (range(0, 4), range(4, 8)):
            left = jnp.concatenate([normed[r, piece] for r in some], axis=1)
            right = jnp.concatenate([wide[r, 1, rows, :] for r in some], axis=0)
            product = jnp.dot(left, right, preferred_element_type=jnp.float32)
            if piece == 0 and some[0] == 0:
                total[...] = product
            else:
                total[...] += product

    def attend(head, low, high):
        for s in range(low // SEQ, high // SEQ):
            part = total[pl.ds(s * SEQ, SEQ), :].astype(jnp.bfloat16)
            query, keys, vals = part[:, :HEAD], part[:, HEAD:2 * HEAD], part[:, 2 * HEAD:]
            scores = lax.dot_general(query, keys, (((1,), (1,)), ((), ())), preferred_element_type=jnp.float32)
            scores = scores * (HEAD ** -0.5)
            expo = jnp.exp(scores - jnp.max(scores, axis=-1, keepdims=True))
            probs = (expo / jnp.sum(expo, axis=-1, keepdims=True)).astype(jnp.bfloat16)
            mixed = jnp.dot(probs, vals, preferred_element_type=jnp.float32)
            ctx[head, col, pl.ds(s * SEQ, SEQ), :] = mixed.astype(jnp.bfloat16)

    def output(head, distance):
        product = None
        for offset in sorted({distance, (NZ - distance) % NZ}):
            r = (z + offset) % NZ
            left = jnp.concatenate([ctx[head, NX * r + i] for i in range(NX)], axis=1)
            right = last[r, head].reshape(NX * HEAD, WIDTH)
            more = jnp.dot(left, right, preferred_element_type=jnp.float32)
            product = more if product is None else product + more
        if head == 0 and distance == 0:
            sums[...] = product + out_bias[...]
        else:
            sums[...] += product

    distances = range(NZ // 2 + 1)
    w0 = sorted({name for piece in range(WQ) for name in need_w[0, piece]})
    before = ["own"]
    plan.step("own", 0.01, lambda: [copy.wait() for copy in own_copies], ["stats_all"], 1)
    for i, part in enumerate(EARLY):
        share = (part[2] - part[0]) / TOK
        for d in distances:
            many = share if d in (0, NZ // 2) else 2 * share
            plan.step(f"n{i}{d}", 0.3 * many, functools.partial(normalize, part, d), ["stats_all", "own"] + need_e[i][d], 1)
            plan.step(f"p{i}{d}", 0.6 * many, functools.partial(project, part, d), w0 + [f"n{i}{d}"] + before, 1)
            before = [f"p{i}{d}"]
        plan.step(f"a{i}", 0.9 * share, functools.partial(attend, 0, part[0], part[2]), before, 0)
    before = [f"a{len(EARLY) - 1}"]
    for piece in range(NX):
        parts = range(piece * WQ // NX, (piece + 1) * WQ // NX)
        needs = [name for part in parts for name in need_w[1, part]]
        plan.step(f"q{piece}", 1.2, functools.partial(project_piece, piece), needs + before, 1)
        before = [f"q{piece}"]
        plan.steps[f"q{piece}"]["eager"] = EAGER if piece == NX - 1 else 0.0
    plan.step("b0", 0.8, functools.partial(attend, 1, 0, TOK), before, 0)
    plan.steps["b0"]["eager"] = EAGER

    for head, parts in enumerate((EARLY, LATE)):
        def ctx_slot(dz, dx, rows, src, head=head):
            place = NX * ((z + dz + NZ) % NZ) + (x + dx + NX) % NX
            return ctx.at[head, place, pl.ds(rows[0], rows[1] - rows[0]), :]

        need_c = [
            gather(plan, f"{'cd'[head]}{i}", ctx_slot, part, HEAD * 2, ["b0" if head else f"a{i}"], LEVELS[1 + head], MERGED[head])
            for i, part in enumerate(parts)
        ]
        before = [f"f{head - 1}{NZ // 2}"] if head else []
        for d in distances:
            many = 1 if d in (0, NZ // 2) else 2
            plan.step(
                f"f{head}{d}", 0.21 * many, functools.partial(output, head, d),
                need_o[head] + [name for need in need_c for name in need[d]] + before, 2,
            )
            before = [f"f{head}{d}"]

    order = plan.order(RATE, LAG)
    sends = dict(
        sx=stat_x.at[pl.ds(0, NX - 1)], sz=stat_z.at[pl.ds(0, NZ - 1)], w=wide.at[pl.ds(0, 7)], o=last.at[pl.ds(0, 7)]
    )
    others = pl.ds(0, NZ * NX - 1)
    for tag, buffer, parts in (("e", raw, EARLY), ("c", ctx.at[0], EARLY), ("d", ctx.at[1], LATE)):
        for i, part in enumerate(parts):
            sends[f"{tag}{i}"] = buffer.at[others, pl.ds(part[0], part[2] - part[0]), :]
    send_index = {name: i for i, name in enumerate(sends)}

    def start(item):
        pltpu.make_async_remote_copy(
            src_ref=item["src"](), dst_ref=item["dst"](), send_sem=send_sem.at[send_index[item["sent"]]],
            recv_sem=recv_sem.at[plan.groups[item["group"]]["index"]],
            device_id=near[item["link"]], device_id_type=MESH,
        ).start()

    def take(ref, sem):
        pltpu.make_async_copy(ref, ref, sem).wait()

    def of_size(size):
        rows = size // (HEAD * 2)
        for slots in range(1, NZ * NX + 1):
            if rows % (16 * slots) == 0 and rows // slots <= TOK:
                return ctx.at[0, pl.ds(0, slots), pl.ds(0, rows // slots)]
        raise ValueError(size)

    barrier = pltpu.get_barrier_semaphore()
    partners = {k: v for k, v in near.items() if k not in ("sx1", "sx3", "sz1", "sz7")}
    for device in partners.values():
        pl.semaphore_signal(barrier, inc=1, device_id=device, device_id_type=MESH)
    own_copies = [
        pltpu.make_async_copy(w_qkv.at[:, pl.ds(0, 384)], wide.at[row, 0], own_sem.at[0]),
        pltpu.make_async_copy(w_qkv.at[:, pl.ds(384, 384)], wide.at[row, 1], own_sem.at[1]),
        pltpu.make_async_copy(w_out.at[:, 0], last.at[row, 0], own_sem.at[2]),
        pltpu.make_async_copy(w_out.at[:, 1], last.at[row, 1], own_sem.at[3]),
    ]
    for item in own_copies:
        item.start()
    pl.semaphore_wait(barrier, len(partners))

    seen = set()
    for name in order:
        item = plan.copies.get(name) or plan.steps[name]
        for need in item["needs"]:
            if need in plan.groups and need not in seen:
                seen.add(need)
                group = plan.groups[need]
                take(of_size(group["size"]), recv_sem.at[group["index"]])
        if name in plan.copies:
            start(item)
        else:
            item["run"]()
    for name, ref in sends.items():
        take(ref, send_sem.at[send_index[name]])
    out[...] = sums[...].astype(jnp.bfloat16)


QUEUE = 1.5
HOP = 0.01
FREE = True
MERGED = (NZ, 3)
EAGER = 1.0
LEVELS = (0, 0, 0)
RATE = dict(x=47e3, y=45e3, z=47e3, c=500e3, s=47e3)
LAG = dict(x=1.8, y=1.8, z=1.8, c=1.0, s=8.0)
GROUPS = 2 + (2 * 2 * WQ + 1 + NX) + 6 + len(EARLY) * (26 + 26 - 5) + len(LATE) * (26 - 2)


def on_device(embeds, ln_gain, ln_bias, w_qkv, w_out, out_bias):
    vmem = pl.BlockSpec(memory_space=pltpu.VMEM)
    anywhere = pl.BlockSpec(memory_space=pl.ANY)
    bf16, f32 = jnp.bfloat16, jnp.float32
    return pl.pallas_call(
        kernel,
        out_shape=jax.ShapeDtypeStruct((TOK, WIDTH), bf16),
        in_specs=[vmem, vmem, vmem, anywhere, anywhere, vmem],
        out_specs=vmem,
        scratch_shapes=[
            pltpu.VMEM((NZ * NX, TOK, WIDTH), bf16),
            pltpu.VMEM((NZ, NX, TOK, WIDTH), bf16),
            pltpu.VMEM((8, 2, 1024, 384), bf16),
            pltpu.VMEM((8, 2, NX, HEAD, WIDTH), bf16),
            pltpu.VMEM((2, NZ * NX, TOK, HEAD), bf16),
            pltpu.VMEM((TOK, 384), f32),
            pltpu.VMEM((TOK, WIDTH), f32),
            pltpu.VMEM((TOK, WIDTH), f32),
            pltpu.VMEM((TOK, WIDTH), f32),
            pltpu.VMEM((NX, 8, TOK), f32),
            pltpu.VMEM((NZ, 8, TOK), f32),
            pltpu.SemaphoreType.DMA((4 + 2 * len(EARLY) + len(LATE),)),
            pltpu.SemaphoreType.DMA((GROUPS,)),
            pltpu.SemaphoreType.DMA((4,)),
        ],
        compiler_params=pltpu.CompilerParams(
            collective_id=0, has_side_effects=True, vmem_limit_bytes=60 * 1024 * 1024
        ),
        name="block",
    )(
        embeds, ln_gain.reshape(1, D), ln_bias.reshape(1, D), w_qkv,
        w_out.reshape(NX, 2, HEAD, WIDTH), out_bias.reshape(1, WIDTH),
    )


def solution(mesh):
    return jax.shard_map(
        on_device,
        mesh=mesh,
        in_specs=(P("row", "col"), P(), P(), P("row", "col"), P("row", "col"), P("col")),
        out_specs=P("row", "col"),
        check_vma=False,
    )
```

```python
import functools
import heapq

import jax
import jax.numpy as jnp
from jax import lax
from jax.experimental import pallas as pl
from jax.experimental.pallas import tpu as pltpu
from jax.sharding import PartitionSpec as P

D = 8192
SEQ = 128
HEAD = 128
TOK = 384
WIDTH = 256
NX, NY, NZ = 4, 4, 8
EARLY = ((0, 96, 256), (256, 320, 384))
LATE = ((0, 96, 256), (256, 320, 384))
AHEAD = 3
WQ = 4
QROWS = 1024 // WQ
MESH = pl.DeviceIdType.MESH


class Plan:
    def __init__(self):
        self.copies = {}
        self.groups = {}
        self.steps = {}

    def copy(self, name, link, size, src, dst, group, sent, needs=(), level=0):
        self.copies[name] = dict(
            link=link, size=size, src=src, dst=dst, group=group, sent=sent, needs=tuple(needs), level=level
        )
        if group not in self.groups:
            self.groups[group] = dict(index=len(self.groups), size=0)
        self.groups[group]["size"] += size

    def step(self, name, cost, run, needs=(), level=0):
        self.steps[name] = dict(cost=cost, run=run, needs=tuple(needs), level=level)

    def order(self, rate, lag):
        now, when, free, left = 0.0, {}, {}, {}
        for item in self.copies.values():
            left[item["group"]] = left.get(item["group"], 0) + 1
        landed = {}
        waiting = {**self.copies, **self.steps}
        result = []
        while waiting:
            best = None
            for name, item in waiting.items():
                times = [when.get(need) for need in item["needs"]]
                if any(t is None for t in times):
                    continue
                ready = max(times, default=0.0)
                if "link" in item:
                    ready = max(ready, free.get(item["link"], 0.0) - QUEUE.get(item["link"][0], 99.0))
                key = (max(ready - item.get("eager", 0.0), now), item["level"], ready, name in self.steps)
                if best is None or key < best[0]:
                    best = (key, name)
            key, name = best
            item = waiting.pop(name)
            now = max(now, key[2])
            result.append(name)
            if name in self.steps:
                now += item["cost"]
                when[name] = now
            else:
                now += 0.01
                link, group = item["link"], item["group"]
                begin = max(now, free.get(link, 0.0))
                free[link] = begin + item["size"] / rate[link[0]]
                landed[group] = max(landed.get(group, 0.0), free[link] + lag[link[0]])
                left[group] -= 1
                if not left[group]:
                    when[group] = landed[group]
        self.when = when
        return result


def halves(rows, mark):
    low, high = rows
    middle = (low + high) // 2
    return (low, middle) if mark == "p" else (middle, high)


def ring(plan, axis, n, tag, classes, slot, rows, size, needs, level, after=0, last=None):
    done = {0: list(needs)}
    for hop in range(1, n // 2 + 1):
        group = last if last and hop == n // 2 else f"{tag}_{hop}"
        for place in classes:
            for sign, mark in ((-1, "p"), (1, "m")):
                part = halves(rows, mark) if hop == n // 2 else rows
                place_of = (place, sign * (hop - 1), part)
                plan.copy(
                    f"{tag}_{place}{mark}{hop}", axis + mark, size * (part[1] - part[0]),
                    functools.partial(slot, *place_of, True), functools.partial(slot, *place_of, False), group,
                    tag[:2], done[hop - 1], level - HOP * (n // 2 - hop + after),
                )
        done[hop] = [group]
    return done


def gather(plan, tag, slot, part, size, needs, level, merged=0):
    first, second = part[:2], part[1:]
    found = {distance: [] for distance in range(NZ // 2 + 1)}
    ends = lambda distance: f"{tag}z" if distance < merged else None
    along_x = lambda place, offset, rows, src: slot(place, offset, rows, src)
    along_z = lambda place, offset, rows, src: slot(offset, place, rows, src)
    pairs = lambda distance, n: sorted({distance, (n - distance) % n})
    across = ring(plan, "x", NX, tag + "a", [0], along_x, first, size, needs, level, NZ // 2)
    along = ring(plan, "z", NZ, tag + "b", [0], along_z, second, size, needs, level, NX // 2)
    for distance in range(NX // 2 + 1):
        done = ring(plan, "z", NZ, f"{tag}a{distance}", pairs(distance, NX), along_z, first, size, across[distance],
                    level, 0, ends(NZ // 2) or f"{tag}al")
        for hop, names in done.items():
            found[hop] += names
    for distance in range(NZ // 2 + 1):
        done = ring(plan, "x", NX, f"{tag}b{distance}", pairs(distance, NZ), along_x, second, size, along[distance],
                    level, 0, ends(distance))
        for names in done.values():
            found[distance] += names
    return found


def to_columns(row):
    wide = jnp.transpose(jnp.broadcast_to(row, (128, TOK)))
    return jnp.concatenate([wide] * (WIDTH // 128), axis=1)


def kernel(embeds, gain, shift, w_qkv, w_out, out_bias, out, raw, normed, wide, last, ctx, total, sums, mean_cols,
           scale_cols, stat_x, stat_z, send_sem, recv_sem, own_sem):
    row, col = lax.axis_index("row"), lax.axis_index("col")
    y, core = row // 2, row % 2
    z, x = col // NX, col % NX

    def at(dx=0, dy=0, dz=0, other=0):
        their_core = 1 - core if other else core
        return (2 * ((y + dy + NY) % NY) + their_core, NX * ((z + dz + NZ) % NZ) + (x + dx + NX) % NX)

    near = dict(
        xp=at(dx=1), xm=at(dx=-1), yp=at(dy=1), ym=at(dy=-1), zp=at(dz=1), zm=at(dz=-1), c=at(other=1)
    )
    for d in range(1, NX):
        near[f"sx{d}"] = at(dx=d)
    for d in range(1, NZ):
        near[f"sz{d}"] = at(dz=d)

    plan = Plan()

    lines = lax.broadcasted_iota(jnp.int32, (8, TOK), 0)

    def pack(total_, spread):
        return jnp.where(lines == 0, total_, jnp.where(lines == 1, spread, 0.0))

    def merge(stats, n, count):
        totals = [stats[i][0:1] for i in range(n)]
        full = functools.reduce(jnp.add, totals)
        mean = full * (1.0 / (n * count))
        spread = functools.reduce(jnp.add, [stats[i][1:2] for i in range(n)])
        apart = functools.reduce(jnp.add, [(t * (1.0 / count) - mean) ** 2 for t in totals])
        return full, mean, spread + count * apart

    def stats_own():
        values = embeds[...].astype(jnp.float32)
        summed = jnp.sum(values, axis=1, keepdims=True)
        apart = values - summed * (1.0 / WIDTH)
        spread = jnp.sum(apart * apart, axis=1, keepdims=True)
        lane = lax.broadcasted_iota(jnp.int32, (TOK, 128), 1)
        both = jnp.where(lane == 0, summed, jnp.where(lane == 1, spread, 0.0))
        stat_x[x] = jnp.transpose(both)[0:8]
        raw[col] = embeds[...]

    def stats_x():
        full, _, spread = merge(stat_x, NX, WIDTH)
        stat_z[z] = pack(full, spread)

    def stats_all():
        _, mean, spread = merge(stat_z, NZ, NX * WIDTH)
        mean_cols[...] = to_columns(mean)
        scale_cols[...] = to_columns(lax.rsqrt(spread * (1.0 / D) + 1e-05))

    plan.step("stats_own", 0.8, stats_own, [], 0.5)
    for d in range(1, NX):
        plan.copy(f"sx{d}", f"sx{d}", 12288, lambda: stat_x.at[x], lambda: stat_x.at[x], "sx", "sx", ["stats_own"], -2)
    plan.step("stats_x", 0.1, stats_x, ["sx"], -2)
    for d in range(1, NZ):
        plan.copy(f"sz{d}", f"sz{d}", 12288, lambda: stat_z.at[z], lambda: stat_z.at[z], "sz", "sz", ["stats_x"], -2)
    plan.step("stats_all", 0.2, stats_all, ["sz"], -2)

    def weights(tag, own, slot, count, unit, gate, from_core):
        whole = (0, count)
        ends = [f"{tag}_1", f"{tag}_2", from_core]
        for mark, sign in (("p", -1), ("m", 1)):
            part = halves(whole, mark)
            plan.copy(f"{tag}_{mark}1", "y" + mark, count * unit, own, functools.partial(slot, 0, whole), ends[0],
                      tag[0], gate, -1)
            near_part, near_all = functools.partial(slot, sign, part), functools.partial(slot, sign, whole)
            far_part = functools.partial(slot, 2 * sign, part)
            plan.copy(f"{tag}_{mark}2", "y" + mark, (part[1] - part[0]) * unit, near_part, near_part, ends[1], tag[0],
                      ends[:1], -1)
            plan.copy(f"{tag}_{mark}1c", "c", count * unit, near_all, near_all, from_core, tag[0], ends[:1], -1)
            plan.copy(f"{tag}_{mark}2c", "c", (part[1] - part[0]) * unit, far_part, far_part, from_core, tag[0],
                      ends[1:2], -1)
        plan.copy(f"{tag}_c", "c", count * unit, own, functools.partial(slot, 0, whole), from_core, tag[0], gate, -1)
        return ends

    def wide_slot(head, piece, dy, rows):
        return wide.at[2 * ((y + dy + NY) % NY) + core, head, pl.ds(piece * QROWS + rows[0], rows[1] - rows[0]), :]

    def last_slot(head, dy, rows):
        return last.at[2 * ((y + dy + NY) % NY) + core, head, pl.ds(rows[0], rows[1] - rows[0])]

    need_w, gates = {}, [[]] * AHEAD

    def gate(head, piece):
        if head and piece < FIRST:
            return [f"w0{WQ - 1 - FIRST + piece}_1"]
        if head and piece < FIRST + NEXT:
            return [f"w0{WQ - 1}_1"]
        return gates[-AHEAD]

    for head in range(2):
        for piece in range(WQ):
            own = lambda head=head, piece=piece: w_qkv.at[pl.ds(piece * QROWS, QROWS), pl.ds(head * 384, 384)]
            need_w[head, piece] = weights(
                f"w{head}{piece}", own, functools.partial(wide_slot, head, piece), QROWS, 768,
                gate(head, piece), f"w1{piece * NX // WQ}_c" if head else "w0_c",
            )
            gates.append([f"w{head}{piece}_1"])
    need_o = {}
    for head in range(2):
        own = lambda head=head: w_out.at[:, head]
        need_o[head] = weights(
            f"o{head}", own, functools.partial(last_slot, head), 4, HEAD * WIDTH * 2, [f"w1{WQ - 1}_1"], f"o{head}_c"
        )

    def raw_slot(dz, dx, rows, src):
        if src and dz == 0 and dx == 0:
            return embeds.at[pl.ds(rows[0], rows[1] - rows[0]), :]
        return raw.at[NX * ((z + dz + NZ) % NZ) + (x + dx + NX) % NX, pl.ds(rows[0], rows[1] - rows[0]), :]

    need_e = [gather(plan, f"e{i}", raw_slot, part, WIDTH * 2, [], LEVELS[0]) for i, part in enumerate(EARLY)]

    def normalize(part, distance):
        rows = pl.ds(part[0], part[2] - part[0])
        for offset in sorted({distance, (NZ - distance) % NZ}):
            r = (z + offset) % NZ

            def body(i, carry, r=r):
                columns = pl.ds(pl.multiple_of((NX * r + i) * WIDTH, WIDTH), WIDTH)
                values = raw[NX * r + i, rows, :].astype(jnp.float32)
                values = (values - mean_cols[rows, :]) * scale_cols[rows, :] * gain[:, columns] + shift[:, columns]
                normed[r, i, rows, :] = values.astype(jnp.bfloat16)
                return carry

            lax.fori_loop(0, NX, body, 0)

    def project(part, distance):
        rows = pl.ds(part[0], part[2] - part[0])
        for offset in sorted({distance, (NZ - distance) % NZ}):
            r = (z + offset) % NZ
            left = jnp.concatenate([normed[r, i, rows, :] for i in range(NX)], axis=1)
            product = jnp.dot(left, wide[r, 0], preferred_element_type=jnp.float32)
            if offset == 0:
                total[rows, :] = product
            else:
                total[rows, :] += product

    def project_piece(piece):
        rows = pl.ds(piece * WIDTH, WIDTH)
        for some in (range(0, 4), range(4, 8)):
            left = jnp.concatenate([normed[r, piece] for r in some], axis=1)
            right = jnp.concatenate([wide[r, 1, rows, :] for r in some], axis=0)
            product = jnp.dot(left, right, preferred_element_type=jnp.float32)
            if piece == 0 and some[0] == 0:
                total[...] = product
            else:
                total[...] += product

    def attend(head, low, high):
        for s in range(low // SEQ, high // SEQ):
            part = total[pl.ds(s * SEQ, SEQ), :].astype(jnp.bfloat16)
            query, keys, vals = part[:, :HEAD], part[:, HEAD:2 * HEAD], part[:, 2 * HEAD:]
            scores = lax.dot_general(query, keys, (((1,), (1,)), ((), ())), preferred_element_type=jnp.float32)
            scores = scores * (HEAD ** -0.5)
            expo = jnp.exp(scores - jnp.max(scores, axis=-1, keepdims=True))
            probs = (expo / jnp.sum(expo, axis=-1, keepdims=True)).astype(jnp.bfloat16)
            mixed = jnp.dot(probs, vals, preferred_element_type=jnp.float32)
            ctx[head, col, pl.ds(s * SEQ, SEQ), :] = mixed.astype(jnp.bfloat16)

    def output(head, distance):
        product = None
        for offset in sorted({distance, (NZ - distance) % NZ}):
            r = (z + offset) % NZ
            left = jnp.concatenate([ctx[head, NX * r + i] for i in range(NX)], axis=1)
            right = last[r, head].reshape(NX * HEAD, WIDTH)
            more = jnp.dot(left, right, preferred_element_type=jnp.float32)
            product = more if product is None else product + more
        if head == 0 and distance == 0:
            sums[...] = product + out_bias[...]
        else:
            sums[...] += product

    distances = range(NZ // 2 + 1)
    w0 = sorted({name for piece in range(WQ) for name in need_w[0, piece]})
    before = ["own"]
    plan.step("own", 0.01, lambda: [copy.wait() for copy in own_copies], ["stats_all"], 1)
    for i, part in enumerate(EARLY):
        share = (part[2] - part[0]) / TOK
        for d in distances:
            many = share if d in (0, NZ // 2) else 2 * share
            plan.step(f"n{i}{d}", 0.3 * many, functools.partial(normalize, part, d), ["stats_all", "own"] + need_e[i][d], 1)
            plan.step(f"p{i}{d}", 0.6 * many, functools.partial(project, part, d), w0 + [f"n{i}{d}"] + before, 1)
            before = [f"p{i}{d}"]
        plan.step(f"a{i}", 0.9 * share, functools.partial(attend, 0, part[0], part[2]), before, 0)
    before = [f"a{len(EARLY) - 1}"]
    for piece in range(NX):
        parts = range(piece * WQ // NX, (piece + 1) * WQ // NX)
        needs = [name for part in parts for name in need_w[1, part]]
        plan.step(f"q{piece}", 1.2, functools.partial(project_piece, piece), needs + before, 1)
        before = [f"q{piece}"]
        plan.steps[f"q{piece}"]["eager"] = EAGER if piece == NX - 1 else 0.0
    plan.step("b0", 0.8, functools.partial(attend, 1, 0, TOK), before, 0)
    plan.steps["b0"]["eager"] = EAGER

    for head, parts in enumerate((EARLY, LATE)):
        def ctx_slot(dz, dx, rows, src, head=head):
            place = NX * ((z + dz + NZ) % NZ) + (x + dx + NX) % NX
            return ctx.at[head, place, pl.ds(rows[0], rows[1] - rows[0]), :]

        need_c = [
            gather(plan, f"{'cd'[head]}{i}", ctx_slot, part, HEAD * 2, ["b0" if head else f"a{i}"], LEVELS[1 + head], MERGED[head])
            for i, part in enumerate(parts)
        ]
        before = [f"f{head - 1}{NZ // 2}"] if head else []
        for d in distances:
            many = 1 if d in (0, NZ // 2) else 2
            plan.step(
                f"f{head}{d}", 0.21 * many, functools.partial(output, head, d),
                need_o[head] + [name for need in need_c for name in need[d]] + before, 2,
            )
            before = [f"f{head}{d}"]

    order = plan.order(RATE, LAG)
    sends = dict(
        sx=stat_x.at[pl.ds(0, NX - 1)], sz=stat_z.at[pl.ds(0, NZ - 1)], w=wide.at[pl.ds(0, 7)], o=last.at[pl.ds(0, 7)]
    )
    others = pl.ds(0, NZ * NX - 1)
    for tag, buffer, parts in (("e", raw, EARLY), ("c", ctx.at[0], EARLY), ("d", ctx.at[1], LATE)):
        for i, part in enumerate(parts):
            sends[f"{tag}{i}"] = buffer.at[others, pl.ds(part[0], part[2] - part[0]), :]
    send_index = {name: i for i, name in enumerate(sends)}

    def start(item):
        pltpu.make_async_remote_copy(
            src_ref=item["src"](), dst_ref=item["dst"](), send_sem=send_sem.at[send_index[item["sent"]]],
            recv_sem=recv_sem.at[plan.groups[item["group"]]["index"]],
            device_id=near[item["link"]], device_id_type=MESH,
        ).start()

    def take(ref, sem):
        pltpu.make_async_copy(ref, ref, sem).wait()

    def of_size(size):
        rows = size // (HEAD * 2)
        for slots in range(1, NZ * NX + 1):
            if rows % (16 * slots) == 0 and rows // slots <= TOK:
                return ctx.at[0, pl.ds(0, slots), pl.ds(0, rows // slots)]
        raise ValueError(size)

    barrier = pltpu.get_barrier_semaphore()
    partners = {k: v for k, v in near.items() if k not in ("sx1", "sx3", "sz1", "sz7")}
    for device in partners.values():
        pl.semaphore_signal(barrier, inc=1, device_id=device, device_id_type=MESH)
    own_copies = [
        pltpu.make_async_copy(w_qkv.at[:, pl.ds(0, 384)], wide.at[row, 0], own_sem.at[0]),
        pltpu.make_async_copy(w_qkv.at[:, pl.ds(384, 384)], wide.at[row, 1], own_sem.at[1]),
        pltpu.make_async_copy(w_out.at[:, 0], last.at[row, 0], own_sem.at[2]),
        pltpu.make_async_copy(w_out.at[:, 1], last.at[row, 1], own_sem.at[3]),
    ]
    for item in own_copies:
        item.start()
    pl.semaphore_wait(barrier, len(partners))

    seen = set()
    for name in order:
        item = plan.copies.get(name) or plan.steps[name]
        for need in item["needs"]:
            if need in plan.groups and need not in seen:
                seen.add(need)
                group = plan.groups[need]
                take(of_size(group["size"]), recv_sem.at[group["index"]])
        if name in plan.copies:
            start(item)
        else:
            item["run"]()
    for name, ref in sends.items():
        take(ref, send_sem.at[send_index[name]])
    out[...] = sums[...].astype(jnp.bfloat16)


QUEUE = dict(x=1.5, z=1.5)
HOP = 0.01
FIRST = 0
NEXT = 0
MERGED = (NZ, 3)
EAGER = 1.0
LEVELS = (0, 0, 0)
RATE = dict(x=47e3, y=45e3, z=47e3, c=500e3, s=47e3)
LAG = dict(x=1.8, y=1.8, z=1.8, c=1.0, s=8.0)
GROUPS = 2 + (2 * 2 * WQ + 1 + NX) + 6 + len(EARLY) * (26 + 26 - 5) + len(LATE) * (26 - 2)


def on_device(embeds, ln_gain, ln_bias, w_qkv, w_out, out_bias):
    vmem = pl.BlockSpec(memory_space=pltpu.VMEM)
    anywhere = pl.BlockSpec(memory_space=pl.ANY)
    bf16, f32 = jnp.bfloat16, jnp.float32
    return pl.pallas_call(
        kernel,
        out_shape=jax.ShapeDtypeStruct((TOK, WIDTH), bf16),
        in_specs=[vmem, vmem, vmem, anywhere, anywhere, vmem],
        out_specs=vmem,
        scratch_shapes=[
            pltpu.VMEM((NZ * NX, TOK, WIDTH), bf16),
            pltpu.VMEM((NZ, NX, TOK, WIDTH), bf16),
            pltpu.VMEM((8, 2, 1024, 384), bf16),
            pltpu.VMEM((8, 2, NX, HEAD, WIDTH), bf16),
            pltpu.VMEM((2, NZ * NX, TOK, HEAD), bf16),
            pltpu.VMEM((TOK, 384), f32),
            pltpu.VMEM((TOK, WIDTH), f32),
            pltpu.VMEM((TOK, WIDTH), f32),
            pltpu.VMEM((TOK, WIDTH), f32),
            pltpu.VMEM((NX, 8, TOK), f32),
            pltpu.VMEM((NZ, 8, TOK), f32),
            pltpu.SemaphoreType.DMA((4 + 2 * len(EARLY) + len(LATE),)),
            pltpu.SemaphoreType.DMA((GROUPS,)),
            pltpu.SemaphoreType.DMA((4,)),
        ],
        compiler_params=pltpu.CompilerParams(
            collective_id=0, has_side_effects=True, vmem_limit_bytes=60 * 1024 * 1024
        ),
        name="block",
    )(
        embeds, ln_gain.reshape(1, D), ln_bias.reshape(1, D), w_qkv,
        w_out.reshape(NX, 2, HEAD, WIDTH), out_bias.reshape(1, WIDTH),
    )


def solution(mesh):
    return jax.shard_map(
        on_device,
        mesh=mesh,
        in_specs=(P("row", "col"), P(), P(), P("row", "col"), P("row", "col"), P("col")),
        out_specs=P("row", "col"),
        check_vma=False,
    )
```

```python
import functools
import heapq

import jax
import jax.numpy as jnp
from jax import lax
from jax.experimental import pallas as pl
from jax.experimental.pallas import tpu as pltpu
from jax.sharding import PartitionSpec as P

D = 8192
SEQ = 128
HEAD = 128
TOK = 384
WIDTH = 256
NX, NY, NZ = 4, 4, 8
EARLY = ((0, 96, 256), (256, 320, 384))
LATE = ((0, 96, 256), (256, 320, 384))
AHEAD = 3
WQ = 4
QROWS = 1024 // WQ
MESH = pl.DeviceIdType.MESH


class Plan:
    def __init__(self):
        self.copies = {}
        self.groups = {}
        self.steps = {}

    def copy(self, name, link, size, src, dst, group, sent, needs=(), level=0):
        self.copies[name] = dict(
            link=link, size=size, src=src, dst=dst, group=group, sent=sent, needs=tuple(needs), level=level
        )
        if group not in self.groups:
            self.groups[group] = dict(index=len(self.groups), size=0)
        self.groups[group]["size"] += size

    def step(self, name, cost, run, needs=(), level=0):
        self.steps[name] = dict(cost=cost, run=run, needs=tuple(needs), level=level)

    def order(self, rate, lag):
        now, when, free, left = 0.0, {}, {}, {}
        for item in self.copies.values():
            left[item["group"]] = left.get(item["group"], 0) + 1
        landed = {}
        waiting = {**self.copies, **self.steps}
        result = []
        while waiting:
            best = None
            for name, item in waiting.items():
                times = [when.get(need) for need in item["needs"]]
                if any(t is None for t in times):
                    continue
                ready = max(times, default=0.0)
                if "link" in item:
                    ready = max(ready, free.get(item["link"], 0.0) - QUEUE.get(item["link"][0], 99.0))
                key = (max(ready - item.get("eager", 0.0), now), item["level"], ready, name in self.steps)
                if best is None or key < best[0]:
                    best = (key, name)
            key, name = best
            item = waiting.pop(name)
            now = max(now, key[2])
            result.append(name)
            if name in self.steps:
                now += item["cost"]
                when[name] = now
            else:
                now += 0.01
                link, group = item["link"], item["group"]
                begin = max(now, free.get(link, 0.0))
                free[link] = begin + item["size"] / rate[link[0]]
                landed[group] = max(landed.get(group, 0.0), free[link] + lag[link[0]] + (SLACK if item["size"] == STAT else 0.0))
                left[group] -= 1
                if not left[group]:
                    when[group] = landed[group]
        self.when = when
        return result


def halves(rows, mark):
    low, high = rows
    middle = (low + high) // 2
    return (low, middle) if mark == "p" else (middle, high)


def ring(plan, axis, n, tag, classes, slot, rows, size, needs, level, after=0, last=None):
    done = {0: list(needs)}
    for hop in range(1, n // 2 + 1):
        group = last if last and hop == n // 2 else f"{tag}_{hop}"
        for place in classes:
            for sign, mark in ((-1, "p"), (1, "m")):
                part = halves(rows, mark) if hop == n // 2 else rows
                place_of = (place, sign * (hop - 1), part)
                plan.copy(
                    f"{tag}_{place}{mark}{hop}", axis + mark, size * (part[1] - part[0]),
                    functools.partial(slot, *place_of, True), functools.partial(slot, *place_of, False), group,
                    tag[:2], done[hop - 1], level - HOP * (n // 2 - hop + after),
                )
        done[hop] = [group]
    return done


def gather(plan, tag, slot, part, size, needs, level, merged=0):
    first, second = part[:2], part[1:]
    found = {distance: [] for distance in range(NZ // 2 + 1)}
    ends = lambda distance: f"{tag}z" if distance < merged else None
    along_x = lambda place, offset, rows, src: slot(place, offset, rows, src)
    along_z = lambda place, offset, rows, src: slot(offset, place, rows, src)
    pairs = lambda distance, n: sorted({distance, (n - distance) % n})
    across = ring(plan, "x", NX, tag + "a", [0], along_x, first, size, needs, level, NZ // 2)
    along = ring(plan, "z", NZ, tag + "b", [0], along_z, second, size, needs, level, NX // 2)
    for distance in range(NX // 2 + 1):
        done = ring(plan, "z", NZ, f"{tag}a{distance}", pairs(distance, NX), along_z, first, size, across[distance],
                    level, 0, ends(NZ // 2) or f"{tag}al")
        for hop, names in done.items():
            found[hop] += names
    for distance in range(NZ // 2 + 1):
        done = ring(plan, "x", NX, f"{tag}b{distance}", pairs(distance, NZ), along_x, second, size, along[distance],
                    level, 0, ends(distance))
        for names in done.values():
            found[distance] += names
    return found


def to_columns(row):
    wide = jnp.transpose(jnp.broadcast_to(row, (128, TOK)))
    return jnp.concatenate([wide] * (WIDTH // 128), axis=1)


def kernel(embeds, gain_in, shift_in, w_qkv, w_out, bias_in, out, gain, shift, out_bias, raw, normed, wide, last, ctx, total, sums, mean_cols,
           scale_cols, stat_x, stat_z, send_sem, recv_sem, own_sem):
    row, col = lax.axis_index("row"), lax.axis_index("col")
    y, core = row // 2, row % 2
    z, x = col // NX, col % NX

    def at(dx=0, dy=0, dz=0, other=0):
        their_core = 1 - core if other else core
        return (2 * ((y + dy + NY) % NY) + their_core, NX * ((z + dz + NZ) % NZ) + (x + dx + NX) % NX)

    near = dict(
        xp=at(dx=1), xm=at(dx=-1), yp=at(dy=1), ym=at(dy=-1), zp=at(dz=1), zm=at(dz=-1), c=at(other=1)
    )

    plan = Plan()

    lines = lax.broadcasted_iota(jnp.int32, (8, TOK), 0)

    def pack(total_, spread):
        return jnp.where(lines == 0, total_, jnp.where(lines == 1, spread, 0.0))

    def merge(stats, n, count):
        totals = [stats[i][0:1] for i in range(n)]
        full = functools.reduce(jnp.add, totals)
        mean = full * (1.0 / (n * count))
        spread = functools.reduce(jnp.add, [stats[i][1:2] for i in range(n)])
        apart = functools.reduce(jnp.add, [(t * (1.0 / count) - mean) ** 2 for t in totals])
        return full, mean, spread + count * apart

    def stats_own():
        own_copies[-1].wait()
        values = raw[col].astype(jnp.float32)
        summed = jnp.sum(values, axis=1, keepdims=True)
        apart = values - summed * (1.0 / WIDTH)
        spread = jnp.sum(apart * apart, axis=1, keepdims=True)
        lane = lax.broadcasted_iota(jnp.int32, (TOK, 128), 1)
        both = jnp.where(lane == 0, summed, jnp.where(lane == 1, spread, 0.0))
        stat_x[x] = jnp.transpose(both)[0:8]

    def stats_x():
        full, _, spread = merge(stat_x, NX, WIDTH)
        stat_z[z] = pack(full, spread)

    def stats_all():
        _, mean, spread = merge(stat_z, NZ, NX * WIDTH)
        mean_cols[...] = to_columns(mean)
        scale_cols[...] = to_columns(lax.rsqrt(spread * (1.0 / D) + 1e-05))

    plan.step("stats_own", 0.8, stats_own, [], 0.5)
    def stat_ring(axis, n, stats, place, needs):
        for hop in range(1, n // 2 + 1):
            for sign, mark in ((-1, "p"), (1, "m")):
                if mark == "p" or hop < n // 2:
                    ref = lambda held=(place + sign * (hop - 1) + n) % n: stats.at[held]
                    plan.copy(f"s{axis}{mark}{hop}", axis + mark, STAT, ref, ref, f"s{axis}_{hop}", f"s{axis}", needs, -2)
            needs = [f"s{axis}_{hop}"]
        return [f"s{axis}_{hop}" for hop in range(1, n // 2 + 1)]

    plan.step("stats_x", 0.1, stats_x, stat_ring("x", NX, stat_x, x, ["stats_own"]), -2)
    plan.step("stats_all", 0.2, stats_all, stat_ring("z", NZ, stat_z, z, ["stats_x"]), 0.5)

    def weights(tag, own, slot, count, unit, gate, from_core):
        whole = (0, count)
        ends = [f"{tag}_1", f"{tag}_2", from_core]
        for mark, sign in (("p", -1), ("m", 1)):
            part = halves(whole, mark)
            plan.copy(f"{tag}_{mark}1", "y" + mark, count * unit, own, functools.partial(slot, 0, whole), ends[0],
                      tag[0], gate, -1)
            near_part, near_all = functools.partial(slot, sign, part), functools.partial(slot, sign, whole)
            far_part = functools.partial(slot, 2 * sign, part)
            plan.copy(f"{tag}_{mark}2", "y" + mark, (part[1] - part[0]) * unit, near_part, near_part, ends[1], tag[0],
                      ends[:1], -1)
            plan.copy(f"{tag}_{mark}1c", "c", count * unit, near_all, near_all, from_core, tag[0], ends[:1], -1)
            plan.copy(f"{tag}_{mark}2c", "c", (part[1] - part[0]) * unit, far_part, far_part, from_core, tag[0],
                      ends[1:2], -1)
        plan.copy(f"{tag}_c", "c", count * unit, own, functools.partial(slot, 0, whole), from_core, tag[0], gate, -1)
        return ends

    def wide_slot(head, piece, dy, rows):
        return wide.at[2 * ((y + dy + NY) % NY) + core, head, pl.ds(piece * QROWS + rows[0], rows[1] - rows[0]), :]

    def last_slot(head, dy, rows):
        return last.at[2 * ((y + dy + NY) % NY) + core, head, pl.ds(rows[0], rows[1] - rows[0])]

    need_w, gates = {}, [[]] * AHEAD

    def gate(head, piece):
        if head and piece < FIRST:
            return [f"w0{WQ - 1 - FIRST + piece}_1"]
        if head and piece < FIRST + NEXT:
            return [f"w0{WQ - 1}_1"]
        return gates[-AHEAD]

    for head in range(2):
        for piece in range(WQ):
            own = lambda head=head, piece=piece: w_qkv.at[pl.ds(piece * QROWS, QROWS), pl.ds(head * 384, 384)]
            need_w[head, piece] = weights(
                f"w{head}{piece}", own, functools.partial(wide_slot, head, piece), QROWS, 768,
                gate(head, piece), f"w1{piece * NX // WQ}_c" if head else "w0_c",
            )
            gates.append([f"w{head}{piece}_1"])
    need_o = {}
    for head in range(2):
        own = lambda head=head: w_out.at[:, head]
        need_o[head] = weights(
            f"o{head}", own, functools.partial(last_slot, head), 4, HEAD * WIDTH * 2, [f"w1{WQ - 1}_1"], f"o{head}_c"
        )

    def raw_slot(dz, dx, rows, src):
        if src and dz == 0 and dx == 0:
            return embeds.at[pl.ds(rows[0], rows[1] - rows[0]), :]
        return raw.at[NX * ((z + dz + NZ) % NZ) + (x + dx + NX) % NX, pl.ds(rows[0], rows[1] - rows[0]), :]

    need_e = [gather(plan, f"e{i}", raw_slot, part, WIDTH * 2, [], LEVELS[0]) for i, part in enumerate(EARLY)]

    def normalize(part, distance):
        rows = pl.ds(part[0], part[2] - part[0])
        for offset in sorted({distance, (NZ - distance) % NZ}):
            r = (z + offset) % NZ

            def body(i, carry, r=r):
                columns = pl.ds(pl.multiple_of((NX * r + i) * WIDTH, WIDTH), WIDTH)
                values = raw[NX * r + i, rows, :].astype(jnp.float32)
                values = (values - mean_cols[rows, :]) * scale_cols[rows, :] * gain[:, columns] + shift[:, columns]
                normed[r, i, rows, :] = values.astype(jnp.bfloat16)
                return carry

            lax.fori_loop(0, NX, body, 0)

    def project(part, distance):
        rows = pl.ds(part[0], part[2] - part[0])
        for offset in sorted({distance, (NZ - distance) % NZ}):
            r = (z + offset) % NZ
            left = jnp.concatenate([normed[r, i, rows, :] for i in range(NX)], axis=1)
            product = jnp.dot(left, wide[r, 0], preferred_element_type=jnp.float32)
            if offset == 0:
                total[rows, :] = product
            else:
                total[rows, :] += product

    def project_piece(piece):
        rows = pl.ds(piece * WIDTH, WIDTH)
        for some in (range(0, 4), range(4, 8)):
            left = jnp.concatenate([normed[r, piece] for r in some], axis=1)
            right = jnp.concatenate([wide[r, 1, rows, :] for r in some], axis=0)
            product = jnp.dot(left, right, preferred_element_type=jnp.float32)
            if piece == 0 and some[0] == 0:
                total[...] = product
            else:
                total[...] += product

    def attend(head, low, high):
        for s in range(low // SEQ, high // SEQ):
            part = total[pl.ds(s * SEQ, SEQ), :].astype(jnp.bfloat16)
            query, keys, vals = part[:, :HEAD], part[:, HEAD:2 * HEAD], part[:, 2 * HEAD:]
            scores = lax.dot_general(query, keys, (((1,), (1,)), ((), ())), preferred_element_type=jnp.float32)
            scores = scores * (HEAD ** -0.5)
            expo = jnp.exp(scores - jnp.max(scores, axis=-1, keepdims=True))
            probs = (expo / jnp.sum(expo, axis=-1, keepdims=True)).astype(jnp.bfloat16)
            mixed = jnp.dot(probs, vals, preferred_element_type=jnp.float32)
            ctx[head, col, pl.ds(s * SEQ, SEQ), :] = mixed.astype(jnp.bfloat16)

    def output(head, distance):
        product = None
        for offset in sorted({distance, (NZ - distance) % NZ}):
            r = (z + offset) % NZ
            left = jnp.concatenate([ctx[head, NX * r + i] for i in range(NX)], axis=1)
            right = last[r, head].reshape(NX * HEAD, WIDTH)
            more = jnp.dot(left, right, preferred_element_type=jnp.float32)
            product = more if product is None else product + more
        if head == 0 and distance == 0:
            sums[...] = product + out_bias[...]
        else:
            sums[...] += product

    distances = range(NZ // 2 + 1)
    w0 = sorted({name for piece in range(WQ) for name in need_w[0, piece]})
    before = ["own"]
    plan.step("own", 0.01, lambda: [copy.wait() for copy in own_copies[:-1]], ["stats_all"], 1)
    for i, part in enumerate(EARLY):
        share = (part[2] - part[0]) / TOK
        for d in distances:
            many = share if d in (0, NZ // 2) else 2 * share
            plan.step(f"n{i}{d}", 0.3 * many, functools.partial(normalize, part, d), ["stats_all", "own"] + need_e[i][d], 1)
            plan.step(f"p{i}{d}", 0.6 * many, functools.partial(project, part, d), w0 + [f"n{i}{d}"] + before, 1)
            before = [f"p{i}{d}"]
        plan.step(f"a{i}", 0.9 * share, functools.partial(attend, 0, part[0], part[2]), before, 0)
    before = [f"a{len(EARLY) - 1}"]
    for piece in range(NX):
        parts = range(piece * WQ // NX, (piece + 1) * WQ // NX)
        needs = [name for part in parts for name in need_w[1, part]]
        plan.step(f"q{piece}", 1.6, functools.partial(project_piece, piece), needs + before, 1)
        before = [f"q{piece}"]
        plan.steps[f"q{piece}"]["eager"] = EAGER if piece == NX - 1 else 0.0
    plan.step("b0", 0.8, functools.partial(attend, 1, 0, TOK), before, 0)
    plan.steps["b0"]["eager"] = EAGER

    for head, parts in enumerate((EARLY, LATE)):
        def ctx_slot(dz, dx, rows, src, head=head):
            place = NX * ((z + dz + NZ) % NZ) + (x + dx + NX) % NX
            return ctx.at[head, place, pl.ds(rows[0], rows[1] - rows[0]), :]

        need_c = [
            gather(plan, f"{'cd'[head]}{i}", ctx_slot, part, HEAD * 2, ["b0" if head else f"a{i}"], LEVELS[1 + head], MERGED[head])
            for i, part in enumerate(parts)
        ]
        before = [f"f{head - 1}{NZ // 2}"] if head else []
        for d in distances:
            many = 1 if d in (0, NZ // 2) else 2
            plan.step(
                f"f{head}{d}", 0.21 * many, functools.partial(output, head, d),
                need_o[head] + [name for need in need_c for name in need[d]] + before, 2,
            )
            before = [f"f{head}{d}"]

    order = plan.order(RATE, LAG)
    sends = dict(
        sx=stat_x.at[pl.ds(0, NX - 1)], sz=stat_z.at[pl.ds(0, NZ - 1)], w=wide.at[pl.ds(0, 7)], o=last.at[pl.ds(0, 7)]
    )
    others = pl.ds(0, NZ * NX - 1)
    for tag, buffer, parts in (("e", raw, EARLY), ("c", ctx.at[0], EARLY), ("d", ctx.at[1], LATE)):
        for i, part in enumerate(parts):
            sends[f"{tag}{i}"] = buffer.at[others, pl.ds(part[0], part[2] - part[0]), :]
    send_index = {name: i for i, name in enumerate(sends)}

    def start(item):
        pltpu.make_async_remote_copy(
            src_ref=item["src"](), dst_ref=item["dst"](), send_sem=send_sem.at[send_index[item["sent"]]],
            recv_sem=recv_sem.at[plan.groups[item["group"]]["index"]],
            device_id=near[item["link"]], device_id_type=MESH,
        ).start()

    def take(ref, sem):
        pltpu.make_async_copy(ref, ref, sem).wait()

    def of_size(size):
        rows = size // (HEAD * 2)
        for slots in range(1, NZ * NX + 1):
            if rows % (16 * slots) == 0 and rows // slots <= TOK:
                return ctx.at[0, pl.ds(0, slots), pl.ds(0, rows // slots)]
        raise ValueError(size)

    barrier = pltpu.get_barrier_semaphore()
    for device in near.values():
        pl.semaphore_signal(barrier, inc=1, device_id=device, device_id_type=MESH)
    own_copies = [
        pltpu.make_async_copy(w_qkv.at[:, pl.ds(0, 384)], wide.at[row, 0], own_sem.at[0]),
        pltpu.make_async_copy(w_qkv.at[:, pl.ds(384, 384)], wide.at[row, 1], own_sem.at[1]),
        pltpu.make_async_copy(w_out.at[:, 0], last.at[row, 0], own_sem.at[2]),
        pltpu.make_async_copy(w_out.at[:, 1], last.at[row, 1], own_sem.at[3]),
        pltpu.make_async_copy(gain_in, gain, own_sem.at[4]),
        pltpu.make_async_copy(shift_in, shift, own_sem.at[5]),
        pltpu.make_async_copy(bias_in, out_bias, own_sem.at[6]),
        pltpu.make_async_copy(embeds, raw.at[col], own_sem.at[7]),
    ]
    for item in own_copies:
        item.start()
    pl.semaphore_wait(barrier, len(near))

    seen = set()
    for name in order:
        item = plan.copies.get(name) or plan.steps[name]
        for need in item["needs"]:
            if need in plan.groups and need not in seen:
                seen.add(need)
                group = plan.groups[need]
                take(of_size(group["size"]), recv_sem.at[group["index"]])
        if name in plan.copies:
            start(item)
        else:
            item["run"]()
    for name, ref in sends.items():
        take(ref, send_sem.at[send_index[name]])
    out[...] = sums[...].astype(jnp.bfloat16)


QUEUE = dict(x=1.5, z=1.5)
HOP = 0.01
FIRST = 0
NEXT = 0
MERGED = (NZ, 3)
EAGER = 2.0
STAT = 8 * TOK * 4
SLACK = 0.5
LEVELS = (0, 0, 0)
RATE = dict(x=47e3, y=47e3, z=47e3, c=500e3, s=47e3)
LAG = dict(x=1.8, y=1.8, z=1.8, c=1.0, s=8.0)
GROUPS = 6 + (2 * 2 * WQ + 1 + NX) + 6 + len(EARLY) * (26 + 26 - 5) + len(LATE) * (26 - 2)


def on_device(embeds, ln_gain, ln_bias, w_qkv, w_out, out_bias):
    vmem = pl.BlockSpec(memory_space=pltpu.VMEM)
    anywhere = pl.BlockSpec(memory_space=pl.ANY)
    bf16, f32 = jnp.bfloat16, jnp.float32
    return pl.pallas_call(
        kernel,
        out_shape=jax.ShapeDtypeStruct((TOK, WIDTH), bf16),
        in_specs=[anywhere] * 6,
        out_specs=vmem,
        scratch_shapes=[
            pltpu.VMEM((1, D), f32),
            pltpu.VMEM((1, D), f32),
            pltpu.VMEM((1, WIDTH), f32),
            pltpu.VMEM((NZ * NX, TOK, WIDTH), bf16),
            pltpu.VMEM((NZ, NX, TOK, WIDTH), bf16),
            pltpu.VMEM((8, 2, 1024, 384), bf16),
            pltpu.VMEM((8, 2, NX, HEAD, WIDTH), bf16),
            pltpu.VMEM((2, NZ * NX, TOK, HEAD), bf16),
            pltpu.VMEM((TOK, 384), f32),
            pltpu.VMEM((TOK, WIDTH), f32),
            pltpu.VMEM((TOK, WIDTH), f32),
            pltpu.VMEM((TOK, WIDTH), f32),
            pltpu.VMEM((NX, 8, TOK), f32),
            pltpu.VMEM((NZ, 8, TOK), f32),
            pltpu.SemaphoreType.DMA((4 + 2 * len(EARLY) + len(LATE),)),
            pltpu.SemaphoreType.DMA((GROUPS,)),
            pltpu.SemaphoreType.DMA((8,)),
        ],
        compiler_params=pltpu.CompilerParams(
            collective_id=0, has_side_effects=True, vmem_limit_bytes=60 * 1024 * 1024
        ),
        name="block",
    )(
        embeds, ln_gain.reshape(1, D), ln_bias.reshape(1, D), w_qkv,
        w_out.reshape(NX, 2, HEAD, WIDTH), out_bias.reshape(1, WIDTH),
    )


def solution(mesh):
    return jax.shard_map(
        on_device,
        mesh=mesh,
        in_specs=(P("row", "col"), P(), P(), P("row", "col"), P("row", "col"), P("col")),
        out_specs=P("row", "col"),
        check_vma=False,
    )
```

```python
import functools
import heapq

import jax
import jax.numpy as jnp
from jax import lax
from jax.experimental import pallas as pl
from jax.experimental.pallas import tpu as pltpu
from jax.sharding import PartitionSpec as P

D = 8192
SEQ = 128
HEAD = 128
TOK = 384
WIDTH = 256
NX, NY, NZ = 4, 4, 8
EARLY = ((0, 96, 256), (256, 320, 384))
LATE = ((0, 96, 256), (256, 320, 384))
AHEAD = 3
WQ = 4
QROWS = 1024 // WQ
MESH = pl.DeviceIdType.MESH


class Plan:
    def __init__(self):
        self.copies = {}
        self.groups = {}
        self.steps = {}

    def copy(self, name, link, size, src, dst, group, sent, needs=(), level=0):
        self.copies[name] = dict(
            link=link, size=size, src=src, dst=dst, group=group, sent=sent, needs=tuple(needs), level=level
        )
        if group not in self.groups:
            self.groups[group] = dict(index=len(self.groups), size=0)
        self.groups[group]["size"] += size

    def step(self, name, cost, run, needs=(), level=0):
        self.steps[name] = dict(cost=cost, run=run, needs=tuple(needs), level=level)

    def order(self, rate, lag):
        now, when, free, left = 0.0, {}, {}, {}
        for item in self.copies.values():
            left[item["group"]] = left.get(item["group"], 0) + 1
        landed = {}
        waiting = {**self.copies, **self.steps}
        result = []
        while waiting:
            best = None
            for name, item in waiting.items():
                times = [when.get(need) for need in item["needs"]]
                if any(t is None for t in times):
                    continue
                ready = max(times, default=0.0)
                if "link" in item:
                    ready = max(ready, free.get(item["link"], 0.0) - QUEUE.get(item["link"][0], 99.0))
                key = (max(ready - item.get("eager", 0.0), now), item["level"], ready, name in self.steps)
                if best is None or key < best[0]:
                    best = (key, name)
            key, name = best
            item = waiting.pop(name)
            now = max(now, key[2])
            result.append(name)
            if name in self.steps:
                now += item["cost"]
                when[name] = now
            else:
                now += 0.01
                link, group = item["link"], item["group"]
                begin = max(now, free.get(link, 0.0))
                free[link] = begin + item["size"] / rate[link[0]]
                landed[group] = max(landed.get(group, 0.0), free[link] + lag[link[0]] + (SLACK if item["size"] == STAT else 0.0))
                left[group] -= 1
                if not left[group]:
                    when[group] = landed[group]
        self.when = when
        return result


def halves(rows, mark):
    low, high = rows
    middle = (low + high) // 2
    return (low, middle) if mark == "p" else (middle, high)


def ring(plan, axis, n, tag, classes, slot, rows, size, needs, level, after=0, last=None):
    done = {0: list(needs)}
    for hop in range(1, n // 2 + 1):
        group = last if last and hop == n // 2 else f"{tag}_{hop}"
        for place in classes:
            for sign, mark in ((-1, "p"), (1, "m")):
                part = halves(rows, mark) if hop == n // 2 else rows
                place_of = (place, sign * (hop - 1), part)
                plan.copy(
                    f"{tag}_{place}{mark}{hop}", axis + mark, size * (part[1] - part[0]),
                    functools.partial(slot, *place_of, True), functools.partial(slot, *place_of, False), group,
                    tag[:2], done[hop - 1], level - HOP * (n // 2 - hop + after),
                )
        done[hop] = [group]
    return done


def gather(plan, tag, slot, part, size, needs, level, merged=0):
    first, second = part[:2], part[1:]
    found = {distance: [] for distance in range(NZ // 2 + 1)}
    ends = lambda distance: f"{tag}z" if distance < merged else None
    along_x = lambda place, offset, rows, src: slot(place, offset, rows, src)
    along_z = lambda place, offset, rows, src: slot(offset, place, rows, src)
    pairs = lambda distance, n: sorted({distance, (n - distance) % n})
    across = ring(plan, "x", NX, tag + "a", [0], along_x, first, size, needs, level, NZ // 2)
    along = ring(plan, "z", NZ, tag + "b", [0], along_z, second, size, needs, level, NX // 2)
    for distance in range(NX // 2 + 1):
        done = ring(plan, "z", NZ, f"{tag}a{distance}", pairs(distance, NX), along_z, first, size, across[distance],
                    level, 0, ends(NZ // 2) or f"{tag}al")
        for hop, names in done.items():
            found[hop] += names
    for distance in range(NZ // 2 + 1):
        done = ring(plan, "x", NX, f"{tag}b{distance}", pairs(distance, NZ), along_x, second, size, along[distance],
                    level, 0, ends(distance))
        for names in done.values():
            found[distance] += names
    return found


def to_columns(row):
    wide = jnp.transpose(jnp.broadcast_to(row, (128, TOK)))
    return jnp.concatenate([wide] * (WIDTH // 128), axis=1)


def kernel(embeds, gain_in, shift_in, w_qkv, w_out, bias_in, out, gain, shift, out_bias, raw, normed, wide, last, ctx, total, sums, mean_cols,
           scale_cols, stat_x, stat_z, send_sem, recv_sem, own_sem):
    row, col = lax.axis_index("row"), lax.axis_index("col")
    y, core = row // 2, row % 2
    z, x = col // NX, col % NX

    def at(dx=0, dy=0, dz=0, other=0):
        their_core = 1 - core if other else core
        return (2 * ((y + dy + NY) % NY) + their_core, NX * ((z + dz + NZ) % NZ) + (x + dx + NX) % NX)

    near = dict(
        xp=at(dx=1), xm=at(dx=-1), yp=at(dy=1), ym=at(dy=-1), zp=at(dz=1), zm=at(dz=-1), c=at(other=1)
    )

    plan = Plan()

    lines = lax.broadcasted_iota(jnp.int32, (8, TOK), 0)

    def pack(total_, spread):
        return jnp.where(lines == 0, total_, jnp.where(lines == 1, spread, 0.0))

    def merge(stats, n, count):
        totals = [stats[i][0:1] for i in range(n)]
        full = functools.reduce(jnp.add, totals)
        mean = full * (1.0 / (n * count))
        spread = functools.reduce(jnp.add, [stats[i][1:2] for i in range(n)])
        apart = functools.reduce(jnp.add, [(t * (1.0 / count) - mean) ** 2 for t in totals])
        return full, mean, spread + count * apart

    def stats_own():
        own_copies[-1].wait()
        values = raw[col].astype(jnp.float32)
        summed = jnp.sum(values, axis=1, keepdims=True)
        apart = values - summed * (1.0 / WIDTH)
        spread = jnp.sum(apart * apart, axis=1, keepdims=True)
        lane = lax.broadcasted_iota(jnp.int32, (TOK, 128), 1)
        both = jnp.where(lane == 0, summed, jnp.where(lane == 1, spread, 0.0))
        stat_x[x] = jnp.transpose(both)[0:8]

    def stats_x():
        full, _, spread = merge(stat_x, NX, WIDTH)
        stat_z[z] = pack(full, spread)

    def stats_all():
        _, mean, spread = merge(stat_z, NZ, NX * WIDTH)
        mean_cols[...] = to_columns(mean)
        scale_cols[...] = to_columns(lax.rsqrt(spread * (1.0 / D) + 1e-05))

    plan.step("stats_own", 0.8, stats_own, [], 0.5)
    def stat_ring(axis, n, stats, place, needs):
        for hop in range(1, n // 2 + 1):
            for sign, mark in ((-1, "p"), (1, "m")):
                if mark == "p" or hop < n // 2:
                    ref = lambda held=(place + sign * (hop - 1) + n) % n: stats.at[held]
                    plan.copy(f"s{axis}{mark}{hop}", axis + mark, STAT, ref, ref, f"s{axis}_{hop}", f"s{axis}", needs, -2)
            needs = [f"s{axis}_{hop}"]
        return [f"s{axis}_{hop}" for hop in range(1, n // 2 + 1)]

    plan.step("stats_x", 0.1, stats_x, stat_ring("x", NX, stat_x, x, ["stats_own"]), -2)
    plan.step("stats_all", 0.2, stats_all, stat_ring("z", NZ, stat_z, z, ["stats_x"]), 0.5)

    def weights(tag, own, slot, count, unit, gate, from_core):
        whole = (0, count)
        ends = [f"{tag}_1", f"{tag}_2", from_core]
        for mark, sign in (("p", -1), ("m", 1)):
            part = halves(whole, mark)
            plan.copy(f"{tag}_{mark}1", "y" + mark, count * unit, own, functools.partial(slot, 0, whole), ends[0],
                      tag[0], gate, -1)
            near_part, near_all = functools.partial(slot, sign, part), functools.partial(slot, sign, whole)
            far_part = functools.partial(slot, 2 * sign, part)
            plan.copy(f"{tag}_{mark}2", "y" + mark, (part[1] - part[0]) * unit, near_part, near_part, ends[1], tag[0],
                      ends[:1], -1)
            plan.copy(f"{tag}_{mark}1c", "c", count * unit, near_all, near_all, from_core, tag[0], ends[:1], -1)
            plan.copy(f"{tag}_{mark}2c", "c", (part[1] - part[0]) * unit, far_part, far_part, from_core, tag[0],
                      ends[1:2], -1)
        plan.copy(f"{tag}_c", "c", count * unit, own, functools.partial(slot, 0, whole), from_core, tag[0], gate, -1)
        return ends

    def wide_slot(head, piece, dy, rows):
        return wide.at[2 * ((y + dy + NY) % NY) + core, head, pl.ds(piece * QROWS + rows[0], rows[1] - rows[0]), :]

    def last_slot(head, dy, rows):
        return last.at[2 * ((y + dy + NY) % NY) + core, head, pl.ds(rows[0], rows[1] - rows[0])]

    need_w, gates = {}, [[]] * AHEAD

    def gate(head, piece):
        if head and piece < FIRST:
            return [f"w0{WQ - 1 - FIRST + piece}_1"]
        if head and piece < FIRST + NEXT:
            return [f"w0{WQ - 1}_1"]
        return gates[-AHEAD]

    for head in range(2):
        for piece in range(WQ):
            own = lambda head=head, piece=piece: w_qkv.at[pl.ds(piece * QROWS, QROWS), pl.ds(head * 384, 384)]
            need_w[head, piece] = weights(
                f"w{head}{piece}", own, functools.partial(wide_slot, head, piece), QROWS, 768,
                gate(head, piece), f"w1{piece * NX // WQ}_c" if head else "w0_c",
            )
            gates.append([f"w{head}{piece}_1"])
    need_o = {}
    for head in range(2):
        own = lambda head=head: w_out.at[:, head]
        need_o[head] = weights(
            f"o{head}", own, functools.partial(last_slot, head), 4, HEAD * WIDTH * 2, [f"w1{WQ - 1}_1"], f"o{head}_c"
        )

    def raw_slot(dz, dx, rows, src):
        if src and dz == 0 and dx == 0:
            return embeds.at[pl.ds(rows[0], rows[1] - rows[0]), :]
        return raw.at[NX * ((z + dz + NZ) % NZ) + (x + dx + NX) % NX, pl.ds(rows[0], rows[1] - rows[0]), :]

    need_e = [gather(plan, f"e{i}", raw_slot, part, WIDTH * 2, [], LEVELS[0]) for i, part in enumerate(EARLY)]

    def normalize(part, distance):
        rows = pl.ds(part[0], part[2] - part[0])
        for offset in sorted({distance, (NZ - distance) % NZ}):
            r = (z + offset) % NZ

            def body(i, carry, r=r):
                columns = pl.ds(pl.multiple_of((NX * r + i) * WIDTH, WIDTH), WIDTH)
                values = raw[NX * r + i, rows, :].astype(jnp.float32)
                values = (values - mean_cols[rows, :]) * scale_cols[rows, :] * gain[:, columns] + shift[:, columns]
                normed[r, i, rows, :] = values.astype(jnp.bfloat16)
                return carry

            lax.fori_loop(0, NX, body, 0)

    def project(part, distance):
        rows = pl.ds(part[0], part[2] - part[0])
        for offset in sorted({distance, (NZ - distance) % NZ}):
            r = (z + offset) % NZ
            left = jnp.concatenate([normed[r, i, rows, :] for i in range(NX)], axis=1)
            product = jnp.dot(left, wide[r, 0], preferred_element_type=jnp.float32)
            if offset == 0:
                total[rows, :] = product
            else:
                total[rows, :] += product

    def project_piece(piece):
        rows = pl.ds(piece * WIDTH, WIDTH)
        for some in (range(0, 4), range(4, 8)):
            left = jnp.concatenate([normed[r, piece] for r in some], axis=1)
            right = jnp.concatenate([wide[r, 1, rows, :] for r in some], axis=0)
            product = jnp.dot(left, right, preferred_element_type=jnp.float32)
            if piece == 0 and some[0] == 0:
                total[...] = product
            else:
                total[...] += product

    def attend(head, low, high):
        for s in range(low // SEQ, high // SEQ):
            part = total[pl.ds(s * SEQ, SEQ), :].astype(jnp.bfloat16)
            query, keys, vals = part[:, :HEAD], part[:, HEAD:2 * HEAD], part[:, 2 * HEAD:]
            scores = lax.dot_general(query, keys, (((1,), (1,)), ((), ())), preferred_element_type=jnp.float32)
            scores = scores * (HEAD ** -0.5)
            expo = jnp.exp(scores - jnp.max(scores, axis=-1, keepdims=True))
            probs = (expo / jnp.sum(expo, axis=-1, keepdims=True)).astype(jnp.bfloat16)
            mixed = jnp.dot(probs, vals, preferred_element_type=jnp.float32)
            ctx[head, col, pl.ds(s * SEQ, SEQ), :] = mixed.astype(jnp.bfloat16)

    def output(head, distance):
        product = None
        for offset in sorted({distance, (NZ - distance) % NZ}):
            r = (z + offset) % NZ
            left = jnp.concatenate([ctx[head, NX * r + i] for i in range(NX)], axis=1)
            right = last[r, head].reshape(NX * HEAD, WIDTH)
            more = jnp.dot(left, right, preferred_element_type=jnp.float32)
            product = more if product is None else product + more
        if head == 0 and distance == 0:
            sums[...] = product + out_bias[...]
        else:
            sums[...] += product

    distances = range(NZ // 2 + 1)
    w0 = sorted({name for piece in range(WQ) for name in need_w[0, piece]})
    before = ["own"]
    plan.step("own", 0.01, lambda: [copy.wait() for copy in own_copies[:-1]], ["stats_all"], 1)
    for i, part in enumerate(EARLY):
        share = (part[2] - part[0]) / TOK
        for d in distances:
            many = share if d in (0, NZ // 2) else 2 * share
            plan.step(f"n{i}{d}", 0.3 * many, functools.partial(normalize, part, d), ["stats_all", "own"] + need_e[i][d], 1)
            plan.step(f"p{i}{d}", 0.6 * many, functools.partial(project, part, d), w0 + [f"n{i}{d}"] + before, 1)
            before = [f"p{i}{d}"]
        plan.step(f"a{i}", 0.9 * share, functools.partial(attend, 0, part[0], part[2]), before, 0)
    before = [f"a{len(EARLY) - 1}"]
    for piece in range(NX):
        parts = range(piece * WQ // NX, (piece + 1) * WQ // NX)
        needs = [name for part in parts for name in need_w[1, part]]
        plan.step(f"q{piece}", 1.6, functools.partial(project_piece, piece), needs + before, 1)
        before = [f"q{piece}"]
        plan.steps[f"q{piece}"]["eager"] = EAGER if piece == NX - 1 else 0.0
    plan.step("b0", 0.8, functools.partial(attend, 1, 0, TOK), before, 0)
    plan.steps["b0"]["eager"] = EAGER

    for head, parts in enumerate((EARLY, LATE)):
        def ctx_slot(dz, dx, rows, src, head=head):
            place = NX * ((z + dz + NZ) % NZ) + (x + dx + NX) % NX
            return ctx.at[head, place, pl.ds(rows[0], rows[1] - rows[0]), :]

        need_c = [
            gather(plan, f"{'cd'[head]}{i}", ctx_slot, part, HEAD * 2, ["b0" if head else f"a{i}"], LEVELS[1 + head], MERGED[head])
            for i, part in enumerate(parts)
        ]
        before = [f"f{head - 1}{NZ // 2}"] if head else []
        for d in distances:
            many = 1 if d in (0, NZ // 2) else 2
            plan.step(
                f"f{head}{d}", 0.21 * many, functools.partial(output, head, d),
                need_o[head] + [name for need in need_c for name in need[d]] + before, 2,
            )
            before = [f"f{head}{d}"]

    order = plan.order(RATE, LAG)
    sends = dict(
        sx=stat_x.at[pl.ds(0, NX - 1)], sz=stat_z.at[pl.ds(0, NZ - 1)], w=wide.at[pl.ds(0, 7)], o=last.at[pl.ds(0, 7)]
    )
    others = pl.ds(0, NZ * NX - 1)
    for tag, buffer, parts in (("e", raw, EARLY), ("c", ctx.at[0], EARLY), ("d", ctx.at[1], LATE)):
        for i, part in enumerate(parts):
            sends[f"{tag}{i}"] = buffer.at[others, pl.ds(part[0], part[2] - part[0]), :]
    send_index = {name: i for i, name in enumerate(sends)}

    def start(item):
        pltpu.make_async_remote_copy(
            src_ref=item["src"](), dst_ref=item["dst"](), send_sem=send_sem.at[send_index[item["sent"]]],
            recv_sem=recv_sem.at[plan.groups[item["group"]]["index"]],
            device_id=near[item["link"]], device_id_type=MESH,
        ).start()

    def take(ref, sem):
        pltpu.make_async_copy(ref, ref, sem).wait()

    def of_size(size):
        rows = size // (HEAD * 2)
        for slots in range(1, NZ * NX + 1):
            if rows % (16 * slots) == 0 and rows // slots <= TOK:
                return ctx.at[0, pl.ds(0, slots), pl.ds(0, rows // slots)]
        raise ValueError(size)

    barrier = pltpu.get_barrier_semaphore()
    for device in near.values():
        pl.semaphore_signal(barrier, inc=1, device_id=device, device_id_type=MESH)
    own_copies = [
        pltpu.make_async_copy(w_qkv.at[:, pl.ds(0, 384)], wide.at[row, 0], own_sem.at[0]),
        pltpu.make_async_copy(w_qkv.at[:, pl.ds(384, 384)], wide.at[row, 1], own_sem.at[1]),
        pltpu.make_async_copy(w_out.at[:, 0], last.at[row, 0], own_sem.at[2]),
        pltpu.make_async_copy(w_out.at[:, 1], last.at[row, 1], own_sem.at[3]),
        pltpu.make_async_copy(gain_in, gain, own_sem.at[4]),
        pltpu.make_async_copy(shift_in, shift, own_sem.at[5]),
        pltpu.make_async_copy(bias_in, out_bias, own_sem.at[6]),
        pltpu.make_async_copy(embeds, raw.at[col], own_sem.at[7]),
    ]
    for item in own_copies:
        item.start()
    pl.semaphore_wait(barrier, len(near))

    seen = set()
    for name in order:
        item = plan.copies.get(name) or plan.steps[name]
        for need in item["needs"]:
            if need in plan.groups and need not in seen:
                seen.add(need)
                group = plan.groups[need]
                take(of_size(group["size"]), recv_sem.at[group["index"]])
        if name in plan.copies:
            start(item)
        else:
            item["run"]()
    for name, ref in sends.items():
        take(ref, send_sem.at[send_index[name]])
    out[...] = sums[...].astype(jnp.bfloat16)


QUEUE = dict(x=1.5, z=1.5)
HOP = 0.01
FIRST = 0
NEXT = 0
MERGED = (NZ, 3)
EAGER = 2.0
STAT = 8 * TOK * 4
SLACK = 0.5
LEVELS = (0, 0, 0)
RATE = dict(x=45e3, y=47e3, z=45e3, c=500e3, s=47e3)
LAG = dict(x=1.8, y=1.8, z=1.8, c=1.0, s=8.0)
GROUPS = 6 + (2 * 2 * WQ + 1 + NX) + 6 + len(EARLY) * (26 + 26 - 5) + len(LATE) * (26 - 2)


def on_device(embeds, ln_gain, ln_bias, w_qkv, w_out, out_bias):
    vmem = pl.BlockSpec(memory_space=pltpu.VMEM)
    anywhere = pl.BlockSpec(memory_space=pl.ANY)
    bf16, f32 = jnp.bfloat16, jnp.float32
    return pl.pallas_call(
        kernel,
        out_shape=jax.ShapeDtypeStruct((TOK, WIDTH), bf16),
        in_specs=[anywhere] * 6,
        out_specs=vmem,
        scratch_shapes=[
            pltpu.VMEM((1, D), f32),
            pltpu.VMEM((1, D), f32),
            pltpu.VMEM((1, WIDTH), f32),
            pltpu.VMEM((NZ * NX, TOK, WIDTH), bf16),
            pltpu.VMEM((NZ, NX, TOK, WIDTH), bf16),
            pltpu.VMEM((8, 2, 1024, 384), bf16),
            pltpu.VMEM((8, 2, NX, HEAD, WIDTH), bf16),
            pltpu.VMEM((2, NZ * NX, TOK, HEAD), bf16),
            pltpu.VMEM((TOK, 384), f32),
            pltpu.VMEM((TOK, WIDTH), f32),
            pltpu.VMEM((TOK, WIDTH), f32),
            pltpu.VMEM((TOK, WIDTH), f32),
            pltpu.VMEM((NX, 8, TOK), f32),
            pltpu.VMEM((NZ, 8, TOK), f32),
            pltpu.SemaphoreType.DMA((4 + 2 * len(EARLY) + len(LATE),)),
            pltpu.SemaphoreType.DMA((GROUPS,)),
            pltpu.SemaphoreType.DMA((8,)),
        ],
        compiler_params=pltpu.CompilerParams(
            collective_id=0, has_side_effects=True, vmem_limit_bytes=60 * 1024 * 1024
        ),
        name="block",
    )(
        embeds, ln_gain.reshape(1, D), ln_bias.reshape(1, D), w_qkv,
        w_out.reshape(NX, 2, HEAD, WIDTH), out_bias.reshape(1, WIDTH),
    )


def solution(mesh):
    return jax.shard_map(
        on_device,
        mesh=mesh,
        in_specs=(P("row", "col"), P(), P(), P("row", "col"), P("row", "col"), P("col")),
        out_specs=P("row", "col"),
        check_vma=False,
    )
```
